128 devices in a mesh: row: 16 (over x, z), col: 4 (over y_hi, core), tm: 2 (over y_lo).
Axes of the slice: x: 4, y: 4 (y_hi: 2, y_lo: 2; y = y_hi * 2 + y_lo), z: 4, core: 2. Of those that a mesh axis runs over, the one named last changes fastest.
Arguments:
- samples: bfloat16 [1024, 16, 2, 4096], P('row', None, 'tm', 'col'), may hold values from -6 to 6
- whitening: bfloat16 [1024, 1024], replicated, may hold values from -0.1875 to 0.1875
- ridge: float32 [2048], P('col'), may hold values from 2 to 20
- slab_start: int32 [1], replicated, may hold values from 0 to 63
- panels: int32 [4], replicated, may hold values from 0 to 3, as said below
Outputs:
- trailing: float32 [131072, 2048], P(('row', 'tm'), 'col')
- factor: bfloat16 [2, 131072, 512], P(None, ('row', 'tm'))
The draws below stay inside these ranges and needn't reach their ends.
Inputs may be any that keep to these rules, and one draw needn't show every extreme that they name: `panels`: each panel index once.
All inputs are finite; a program needn't handle non-finite values.
Results may differ from the reference program's by a relative error of at most 0.012.
The reference program's roundings to bfloat16 on the way count: a program that leaves them out, or rounds other values in their place, can miss the bound.
Values may be sent and summed in bfloat16 or wider, within the bound.
No kernel may reach another device: no remote copies, remote signals or barrier semaphores. Data moves between devices by JAX's collectives and lax.ppermute only.
A program may use at most 192 MiB of HBM per device.

```python
import math
import jax
import jax.numpy as jnp
from jax import lax

K = 131072
S = 1024
PANEL = 512
PANELS = 2
SLAB = 2048
KD = 4096
N_ROW = 16
N_COL = 4
N_TM = 2


def draw_panels(key, part):
    scored = jax.random.fold_in(key, 9173)
    scores = jax.random.randint(scored, (N_COL,), 0, 1 << 20) * N_COL + jnp.arange(N_COL, dtype=jnp.int32)
    return jnp.argsort(scores, stable=True).astype(jnp.int32)


def steps_of(stream_key, dims, cuts, low, largest):
    level, own = 1.0, jax.random.fold_in(stream_key, 6)
    for position, shards_of in cuts:
        steps = jnp.exp(jax.random.uniform(jax.random.fold_in(own, position), (shards_of,), jnp.float32, low / len(cuts), largest / len(cuts)))
        level = level * jnp.repeat(steps, dims[position] // shards_of).reshape([-1 if axis == position else 1 for axis in range(len(dims))])
    return level


def centred(key, shape, spread, bound, split=(), kind=jnp.bfloat16):
    level = steps_of(key, shape, split, -0.22, 0.18) if split else 1.0
    values = jax.random.normal(key, shape, jnp.float32) * spread * level
    return jnp.minimum(jnp.maximum(values, -bound), bound).astype(kind)


def setup_inputs(seed: int = 0) -> dict:
    keys = jax.random.split(jax.random.key(seed), 6)
    samples = centred(keys[0], (S, N_ROW, N_TM, KD), 1.0, 6.0, ((0, 16), (2, 2), (3, 4)))
    whitening = centred(keys[1], (S, S), S ** -0.5, 0.1875)
    ridge = jnp.clip(jnp.exp(math.log(20.0) - 2.3025851 * jax.random.uniform(keys[2], (SLAB,), jnp.float32) ** steps_of(keys[2], (SLAB,), ((0, 4),), -0.2, 0.2)), 2.0, 20.0)
    slab_start = jax.random.randint(keys[3], (1,), 0, K // SLAB).astype(jnp.int32)
    panels = draw_panels(jax.random.fold_in(keys[5], 71), 0)
    return {"samples": samples, "whitening": whitening, "ridge": ridge, "slab_start": slab_start, "panels": panels}


def reference(samples, whitening, ridge, slab_start, panels):
    flat_data = samples.reshape(S, K)
    whitened = jnp.dot(whitening.astype(jnp.float32), flat_data.astype(jnp.float32), preferred_element_type=jnp.float32).astype(jnp.bfloat16)
    slab_first = (slab_start[0] * SLAB).astype(jnp.int32)
    slab_data = lax.dynamic_slice_in_dim(whitened, slab_first, SLAB, 1)
    covariance = lax.dot_general(whitened.astype(jnp.float32), slab_data.astype(jnp.float32), (((0,), (0,)), ((), ())), preferred_element_type=jnp.float32) * (1.0 / math.sqrt(S))
    zero_index = jnp.zeros((), jnp.int32)
    diag_block = lax.dynamic_slice(covariance, (slab_first, zero_index), (SLAB, SLAB)) + jnp.diag(ridge)
    covariance = lax.dynamic_update_slice(covariance, diag_block, (slab_first, zero_index))
    factors = []
    for section in range(PANELS):
        panel_first = (panels[section] * PANEL).astype(jnp.int32)
        pivot_rows = lax.dynamic_slice_in_dim(covariance, slab_first + panel_first, PANEL, 0)
        pivot_diag = lax.dynamic_slice_in_dim(pivot_rows, panel_first, PANEL, 1)
        lower_factor = jnp.linalg.cholesky(pivot_diag)
        panel_columns = lax.dynamic_slice_in_dim(covariance, panel_first, PANEL, 1)
        panel_now = jax.scipy.linalg.solve_triangular(lower_factor, panel_columns.T, lower=True).T.astype(jnp.bfloat16)
        coupling = jax.scipy.linalg.solve_triangular(lower_factor, pivot_rows, lower=True).T.astype(jnp.bfloat16)
        covariance = covariance - lax.dot_general(panel_now.astype(jnp.float32), coupling.astype(jnp.float32), (((1,), (1,)), ((), ())), preferred_element_type=jnp.float32)
        factors.append(panel_now)
    column_panel = jnp.arange(SLAB) // PANEL
    finished = column_panel == panels[0]
    for section in range(1, PANELS):
        finished = finished | (column_panel == panels[section])
    trailing = jnp.where(finished[None, :], jnp.zeros((), covariance.dtype), covariance)
    return (trailing, jnp.stack(factors))
```

```python
import jax
import jax.numpy as jnp
from jax import lax
from jax.experimental import pallas as pl
from jax.experimental.pallas import tpu as pltpu
from jax.sharding import PartitionSpec as P

S = 1024
PANEL = 512
TILE = 512
HIGH = lax.Precision.HIGHEST


def place(y, core):
    return ((y // 2) * 2 + core) * 2 + y % 2


def y_shift(k):
    return [(place(y, m), place((y + k) % 4, m)) for y in range(4) for m in range(2)]


def x_shift(k):
    return [(x * 4 + z, ((x + k) % 4) * 4 + z) for x in range(4) for z in range(4)]


def z_shift(k):
    return [(x * 4 + z, x * 4 + (z + k) % 4) for x in range(4) for z in range(4)]


def swap(value, bit):
    return lax.ppermute(value, "col", [(c, c ^ bit) for c in range(4)])


def ring_gather(piece, axis, shift, own):
    full = jnp.zeros((4,) + piece.shape, piece.dtype)
    full = lax.dynamic_update_index_in_dim(full, piece, own, 0)
    for k in range(1, 4):
        got = lax.ppermute(piece, axis, shift(k))
        full = lax.dynamic_update_index_in_dim(full, got, (own - k) % 4, 0)
    return full


def dot_t(a, b):
    return lax.dot_general(a, b, (((0,), (0,)), ((), ())), preferred_element_type=jnp.float32)


def dot_tf(a, b):
    return lax.dot_general(a, b, (((0,), (0,)), ((), ())), precision=HIGH)


def dot_nt(a, b):
    return lax.dot_general(a, b, (((1,), (1,)), ((), ())), precision=HIGH)


def split(value):
    high = value.astype(jnp.bfloat16)
    return high, (value - high.astype(jnp.float32)).astype(jnp.bfloat16)


def finish_kernel(
    info, x0, x1, x2, x3, w0h, w0l, w1h, w1l, vh, vl, sc, f0, f1, r0, r1, dc, t_ref, f_ref, x
):
    i = pl.program_id(0)
    for m, source in enumerate((x0, x1, x2, x3)):
        @pl.when(i // 2 == m)
        def _(source=source):
            x[...] = source[...]

    tile = (info[0] ^ (i // 2)) * 2 + i % 2
    xs = x[...]

    def dot(a, b):
        return jnp.dot(a, b[...], preferred_element_type=jnp.float32)

    on0 = (tile == info[1]).astype(jnp.float32)
    on1 = (tile == info[2]).astype(jnp.float32)
    p0 = (dot(xs, w0h) + dot(xs, w0l)) * (1.0 / 32.0) + on0 * r0[...]
    p0 = p0.astype(jnp.bfloat16)
    f_ref[0] = p0
    p1 = (dot(xs, w1h) + dot(xs, w1l)) * (1.0 / 32.0) - (dot(p0, vh) + dot(p0, vl)) + on1 * r1[...]
    p1 = p1.astype(jnp.bfloat16)
    f_ref[1] = p1

    @pl.when(info[4] == 1)
    def _():
        t_ref[...] = jnp.zeros_like(t_ref)

    @pl.when(info[4] == 0)
    def _():
        onc = (tile == info[3]).astype(jnp.float32)
        diagonal = lax.broadcasted_iota(jnp.int32, (TILE, PANEL), 0) == lax.broadcasted_iota(
            jnp.int32, (TILE, PANEL), 1
        )
        add = jnp.where(diagonal, onc * dc[...], 0.0)
        t_ref[...] = dot(xs, sc) * (1.0 / 32.0) + add - dot(p0, f0) - dot(p1, f1)


def finish(info, xs, consts):
    def tile(i, info):
        return (info[0] ^ (i // 2)) * 2 + i % 2

    def x_spec(m):
        return pl.BlockSpec(
            (TILE, S), lambda i, info: (jnp.where(i // 2 == m, i % 2, jnp.where(i // 2 < m, 0, 1)), 0)
        )

    def const_spec(value):
        return pl.BlockSpec(value.shape, lambda i, info: (0, 0), pipeline_mode=pl.Buffered(1))

    return pl.pallas_call(
        finish_kernel,
        out_shape=(
            jax.ShapeDtypeStruct((4 * S, PANEL), jnp.float32),
            jax.ShapeDtypeStruct((2, 4 * S, PANEL), jnp.bfloat16),
        ),
        grid_spec=pltpu.PrefetchScalarGridSpec(
            num_scalar_prefetch=1,
            grid=(8,),
            in_specs=[x_spec(m) for m in range(4)] + [const_spec(v) for v in consts],
            out_specs=(
                pl.BlockSpec((TILE, PANEL), lambda i, info: (tile(i, info), 0)),
                pl.BlockSpec((2, TILE, PANEL), lambda i, info: (0, tile(i, info), 0)),
            ),
            scratch_shapes=[pltpu.VMEM((TILE, S), jnp.bfloat16)],
        ),
        compiler_params=pltpu.CompilerParams(vmem_limit_bytes=44 << 20),
        name="finish",
    )(info, *xs, *consts)


def inverse_factor(a):
    lower = jnp.linalg.cholesky(a)
    return jax.scipy.linalg.solve_triangular(lower, jnp.eye(PANEL, dtype=jnp.float32), lower=True)


def on_device(samples, whitening, ridge, slab_start, panels):
    col = lax.axis_index("col")
    tm = lax.axis_index("tm")
    row = lax.axis_index("row")
    core = col % 2
    y = (col // 2) * 2 + tm
    slab = slab_start[0]
    half, owner_tm, owner_row = slab % 2, (slab // 2) % 2, slab // 4
    local = samples[:, :, 0, :]

    ridges = jnp.zeros((4, PANEL), jnp.float32)
    ridges = lax.dynamic_update_index_in_dim(ridges, ridge, col, 0)
    for bit in (1, 2, 3):
        ridges = lax.dynamic_update_index_in_dim(ridges, swap(ridge, bit), col ^ bit, 0)
    q0, q1 = panels[0], panels[1]
    ridge0 = lax.dynamic_index_in_dim(ridges, q0, 0, keepdims=False)
    ridge1 = lax.dynamic_index_in_dim(ridges, q1, 0, keepdims=False)

    mine = lax.dynamic_index_in_dim(local, owner_row, 1, keepdims=False)
    away = (y - (half * 2 + owner_tm)) % 4
    part = mine
    for k in range(1, 4):
        got = lax.ppermute(mine, ("col", "tm"), y_shift(k))
        part = jnp.where(away == k, got, part)
    line = ring_gather(part, "row", x_shift, row // 4)
    plane = ring_gather(line, "row", z_shift, row % 4)
    raw = plane.transpose(1, 0, 2, 3).reshape(S, S)
    half_slab = jnp.dot(whitening, raw, preferred_element_type=jnp.float32).astype(jnp.bfloat16)
    other = swap(half_slab, 1)
    slabs = jnp.zeros((2, S, S), jnp.bfloat16)
    slabs = lax.dynamic_update_index_in_dim(slabs, half_slab, core, 0)
    slabs = lax.dynamic_update_index_in_dim(slabs, other, 1 - core, 0)

    def panel_of(q):
        return lax.dynamic_slice(slabs, (q // 2, 0, (q % 2) * PANEL), (1, S, PANEL))[0]

    s0, s1, sc = panel_of(q0), panel_of(q1), panel_of(col)

    moved = lax.all_to_all(local, "row", split_axis=1, concat_axis=0, tiled=True)
    series = moved.reshape(S, S)
    own = lax.dot_general(
        series, whitening, (((0,), (1,)), ((), ())), preferred_element_type=jnp.float32
    ).astype(jnp.bfloat16)
    far = swap(own, 2)
    xs = (own, swap(own, 1), far, swap(far, 1))

    scale = 1.0 / 32.0
    a = dot_t(s0, s0) * scale + jnp.diag(ridge0)
    b = dot_t(s0, s1) * scale
    d = dot_t(s1, s1) * scale + jnp.diag(ridge1)
    e0 = dot_t(s0, sc) * scale
    e1 = dot_t(s1, sc) * scale
    inv0 = inverse_factor(a)
    u = jnp.dot(inv0, b, precision=HIGH).astype(jnp.bfloat16)
    f0 = jnp.dot(inv0, e0, precision=HIGH).astype(jnp.bfloat16)
    inv1 = inverse_factor(d - dot_t(u, u))
    f1 = jnp.dot(inv1, e1 - dot_t(u, f0), precision=HIGH).astype(jnp.bfloat16)
    w0 = split(dot_nt(s0.astype(jnp.float32), inv0))
    w1 = split(dot_nt(s1.astype(jnp.float32), inv1))
    v = split(dot_nt(u.astype(jnp.float32), inv1))
    r0 = ridge0[:, None] * inv0.T
    r1 = ridge1[:, None] * inv1.T

    holds = (row == owner_row) & (tm == owner_tm)
    first = half * 4
    done = (col == q0) | (col == q1)

    def slab_tile(q):
        return jnp.where(holds, first + q, -1)

    info = jnp.stack([col, slab_tile(q0), slab_tile(q1), slab_tile(col), done.astype(jnp.int32)])
    consts = (*w0, *w1, *v, sc, f0, f1, r0, r1, ridge[None, :])
    return finish(info.astype(jnp.int32), xs, consts)


def solution(mesh):
    in_specs = (P("row", None, "tm", "col"), P(), P("col"), P(), P())
    out_specs = (P(("row", "tm"), "col"), P(None, ("row", "tm"), None))
    return jax.shard_map(
        on_device, mesh=mesh, in_specs=in_specs, out_specs=out_specs, check_vma=False
    )
```

```python
import jax
import jax.numpy as jnp
from jax import lax
from jax.experimental import pallas as pl
from jax.experimental.pallas import tpu as pltpu
from jax.sharding import PartitionSpec as P

S = 1024
PANEL = 512
TILE = 512
BLOCK = 128
SCALE = 1.0 / 32.0
HIGH = lax.Precision.HIGHEST
F32 = jnp.float32
BF16 = jnp.bfloat16


def place(y, core):
    return ((y // 2) * 2 + core) * 2 + y % 2


def y_shift(k):
    return [(place(y, m), place((y + k) % 4, m)) for y in range(4) for m in range(2)]


def x_shift(k):
    return [(x * 4 + z, ((x + k) % 4) * 4 + z) for x in range(4) for z in range(4)]


def z_shift(k):
    return [(x * 4 + z, x * 4 + (z + k) % 4) for x in range(4) for z in range(4)]


def swap(value, bit):
    return lax.ppermute(value, "col", [(c, c ^ bit) for c in range(4)])


def ring_gather(piece, axis, shift, own):
    full = jnp.zeros((4,) + piece.shape, piece.dtype)
    full = lax.dynamic_update_index_in_dim(full, piece, own, 0)
    for k in range(1, 4):
        got = lax.ppermute(piece, axis, shift(k))
        full = lax.dynamic_update_index_in_dim(full, got, (own - k) % 4, 0)
    return full


def dot_nn(a, b):
    return jnp.dot(a, b, preferred_element_type=F32)


def dot_tn(a, b, precision=None):
    return lax.dot_general(
        a, b, (((0,), (0,)), ((), ())), precision=precision, preferred_element_type=F32
    )


def dot_nt(a, b):
    return lax.dot_general(a, b, (((1,), (1,)), ((), ())), preferred_element_type=F32)


def halves(value):
    high = value.astype(BF16)
    return high, (value - high.astype(F32)).astype(BF16)


def thirds(value):
    high = value.astype(BF16).astype(F32)
    rest = value - high
    middle = rest.astype(BF16).astype(F32)
    return high, middle, rest - middle


def outer(rows):
    h, m, l = thirds(rows)
    w = BLOCK
    left = jnp.concatenate([h[:, :w], h[:, :w], m[:, :w], m[:, :w], h[:, :w], l[:, :w]], 0)
    right = jnp.concatenate([h, m, h, m, l, h], 0)
    return dot_tn(left.astype(BF16), right.astype(BF16))


def factor_block(w):
    sub = lax.broadcasted_iota(jnp.int32, (8, BLOCK), 0)
    for k in range(0, BLOCK, 8):
        left = w[k : k + 8, :BLOCK]
        right = w[k : k + 8, BLOCK:]
        d = {}
        for j in range(8):
            column = jnp.broadcast_to(left[:, k + j : k + j + 1], (8, BLOCK))
            for i in range(j, 8):
                d[i, j] = jnp.broadcast_to(column[i : i + 1, :], (8, BLOCK))
        lefts, rights = [], []
        new_left = jnp.zeros((8, BLOCK), F32)
        new_right = jnp.zeros((8, BLOCK), F32)
        for j in range(8):
            r = lax.rsqrt(d[j, j])
            for i in range(j + 1, 8):
                d[i, j] = d[i, j] * r
            for i in range(j + 1, 8):
                for n in range(i, 8):
                    d[n, i] = d[n, i] - d[n, j] * d[i, j]
            a = jnp.broadcast_to(left[j : j + 1, :], (8, BLOCK))
            b = jnp.broadcast_to(right[j : j + 1, :], (8, BLOCK))
            for i in range(j):
                a = a - d[j, i] * lefts[i]
                b = b - d[j, i] * rights[i]
            lefts.append(a * r)
            rights.append(b * r)
            new_left = jnp.where(sub == j, lefts[j], new_left)
            new_right = jnp.where(sub == j, rights[j], new_right)
        w[k : k + 8, :BLOCK] = new_left
        w[k : k + 8, BLOCK:] = new_right
        if k + 8 < BLOCK:
            update = outer(jnp.concatenate([new_left, new_right], 1))
            w[k + 8 :, :] = w[k + 8 :, :] - update[k + 8 :, :]


def eye(n):
    return lax.broadcasted_iota(jnp.int32, (n, n), 0) == lax.broadcasted_iota(jnp.int32, (n, n), 1)


def eliminate(m, w):
    extra = m.shape[1] - PANEL
    for r0 in range(0, PANEL, BLOCK):
        r1 = r0 + BLOCK
        w[:, :BLOCK] = m[r0:r1, r0:r1]
        w[:, BLOCK:] = eye(BLOCK).astype(F32)
        factor_block(w)
        rows = jnp.dot(w[:, BLOCK:], m[r0:r1, r1 : extra + r1], precision=HIGH)
        m[r0:r1, r1 : extra + r1] = rows
        if r1 < PANEL:
            m[r1:, r1 : extra + r1] -= dot_tn(rows[:, : PANEL - r1], rows, HIGH)


def chain_kernel(s0, s1, g0, g1, inv0, u, inv1, m0, m1, w):
    unit = eye(PANEL)
    m0[:, :PANEL] = dot_tn(s0[...], s0[...]) * SCALE + jnp.where(unit, g0[...], 0.0)
    m0[:, PANEL : 2 * PANEL] = dot_tn(s0[...], s1[...]) * SCALE
    m0[:, 2 * PANEL :] = unit.astype(F32)
    eliminate(m0, w)
    inv0[...] = m0[:, 2 * PANEL :]
    joint = m0[:, PANEL : 2 * PANEL].astype(BF16)
    u[...] = joint
    pivot = dot_tn(s1[...], s1[...]) * SCALE + jnp.where(unit, g1[...], 0.0)
    m1[:, :PANEL] = pivot - dot_tn(joint, joint)
    m1[:, PANEL:] = unit.astype(F32)
    eliminate(m1, w)
    inv1[...] = m1[:, PANEL:]


def chain(s0, s1, g0, g1):
    square = jax.ShapeDtypeStruct((PANEL, PANEL), F32)
    vmem = pl.BlockSpec(memory_space=pltpu.VMEM)
    return pl.pallas_call(
        chain_kernel,
        out_shape=(square, jax.ShapeDtypeStruct((PANEL, PANEL), BF16), square),
        in_specs=[vmem] * 4,
        out_specs=(vmem, vmem, vmem),
        scratch_shapes=[
            pltpu.VMEM((PANEL, 3 * PANEL), F32),
            pltpu.VMEM((PANEL, 2 * PANEL), F32),
            pltpu.VMEM((BLOCK, 2 * BLOCK), F32),
        ],
        compiler_params=pltpu.CompilerParams(vmem_limit_bytes=32 << 20),
        cost_estimate=pl.CostEstimate(flops=80 * 10**9, transcendentals=0, bytes_accessed=5 << 20),
        name="chain",
    )(s0, s1, g0, g1)


def finish_kernel(
    info, x0, x1, x2, x3, s0, s1, sc, inv0, u, inv1, g0, g1, gc, t_ref, f_ref,
    x, w0, w1, v, f0, f1,
):
    i = pl.program_id(0)

    @pl.when(i == 0)
    def _():
        h0, l0 = halves(inv0[...])
        h1, l1 = halves(inv1[...])
        w0[...] = (dot_nt(s0[...], h0) + dot_nt(s0[...], l0)).astype(BF16)
        w1[...] = (dot_nt(s1[...], h1) + dot_nt(s1[...], l1)).astype(BF16)
        v[...] = (dot_nt(u[...], h1) + dot_nt(u[...], l1)).astype(BF16)
        eh, el = halves(dot_tn(s0[...], sc[...]) * SCALE)
        c0 = (dot_nn(h0, eh) + dot_nn(h0, el) + dot_nn(l0, eh)).astype(BF16)
        f0[...] = c0
        eh, el = halves(dot_tn(s1[...], sc[...]) * SCALE - dot_tn(u[...], c0))
        f1[...] = (dot_nn(h1, eh) + dot_nn(h1, el) + dot_nn(l1, eh)).astype(BF16)

    for m, source in enumerate((x0, x1, x2, x3)):
        @pl.when(i // 2 == m)
        def _(source=source):
            x[...] = source[...]

    tile = (info[0] ^ (i // 2)) * 2 + i % 2
    xs = x[...]

    f_ref[0] = (dot_nn(xs, w0[...]) * SCALE).astype(BF16)

    @pl.when(tile == info[1])
    def _():
        ridge = jnp.where(eye(PANEL), g0[...], 0.0)
        add = lax.dot_general(ridge, inv0[...], (((1,), (1,)), ((), ())), precision=HIGH)
        f_ref[0] = (dot_nn(xs, w0[...]) * SCALE + add).astype(BF16)

    p0 = f_ref[0]
    base = dot_nn(xs, w1[...]) * SCALE - dot_nn(p0, v[...])
    f_ref[1] = base.astype(BF16)

    @pl.when(tile == info[2])
    def _():
        ridge = jnp.where(eye(PANEL), g1[...], 0.0)
        add = lax.dot_general(ridge, inv1[...], (((1,), (1,)), ((), ())), precision=HIGH)
        f_ref[1] = (dot_nn(xs, w1[...]) * SCALE - dot_nn(p0, v[...]) + add).astype(BF16)

    @pl.when(info[4] == 1)
    def _():
        t_ref[...] = jnp.zeros_like(t_ref)

    @pl.when(info[4] == 0)
    def _():
        on = (tile == info[3]).astype(F32)
        add = jnp.where(eye(PANEL), on * gc[...], 0.0)
        t_ref[...] = (
            dot_nn(xs, sc[...]) * SCALE + add - dot_nn(p0, f0[...]) - dot_nn(f_ref[1], f1[...])
        )


def finish(info, xs, consts):
    def tile(i, info):
        return (info[0] ^ (i // 2)) * 2 + i % 2

    def x_spec(m):
        return pl.BlockSpec(
            (TILE, S), lambda i, info: (jnp.where(i // 2 == m, i % 2, jnp.where(i // 2 < m, 0, 1)), 0)
        )

    def const_spec(value):
        return pl.BlockSpec(value.shape, lambda i, info: (0, 0), pipeline_mode=pl.Buffered(1))

    return pl.pallas_call(
        finish_kernel,
        out_shape=(
            jax.ShapeDtypeStruct((4 * S, PANEL), F32),
            jax.ShapeDtypeStruct((2, 4 * S, PANEL), BF16),
        ),
        grid_spec=pltpu.PrefetchScalarGridSpec(
            num_scalar_prefetch=1,
            grid=(8,),
            in_specs=[x_spec(m) for m in range(4)] + [const_spec(value) for value in consts],
            out_specs=(
                pl.BlockSpec((TILE, PANEL), lambda i, info: (tile(i, info), 0)),
                pl.BlockSpec((2, TILE, PANEL), lambda i, info: (0, tile(i, info), 0)),
            ),
            scratch_shapes=[
                pltpu.VMEM((TILE, S), BF16),
                pltpu.VMEM((S, PANEL), BF16),
                pltpu.VMEM((S, PANEL), BF16),
                pltpu.VMEM((PANEL, PANEL), BF16),
                pltpu.VMEM((PANEL, PANEL), BF16),
                pltpu.VMEM((PANEL, PANEL), BF16),
            ],
        ),
        compiler_params=pltpu.CompilerParams(vmem_limit_bytes=44 << 20),
        name="finish",
    )(info, *xs, *consts)


def on_device(samples, whitening, ridge, slab_start, panels):
    col = lax.axis_index("col")
    tm = lax.axis_index("tm")
    row = lax.axis_index("row")
    core = col % 2
    y = (col // 2) * 2 + tm
    slab = slab_start[0]
    half, owner_tm, owner_row = slab % 2, (slab // 2) % 2, slab // 4
    q0, q1 = panels[0], panels[1]
    local = samples[:, :, 0, :]

    def pair(value, bit):
        other = swap(value, bit)
        upper = (col & bit) != 0
        return jnp.stack([jnp.where(upper, other, value), jnp.where(upper, value, other)])

    mine = lax.dynamic_index_in_dim(local, owner_row, 1, keepdims=False)
    chip = pair(mine, 1)

    def panel_of(values, q):
        start = (q // 2, 0, (q % 2) * PANEL)
        return lax.dynamic_slice(values, start, (1, values.shape[1], PANEL))[0]

    wanted = jnp.stack([panel_of(chip, jnp.where(core == 0, q0, q1)), panel_of(chip, core), panel_of(chip, core + 2)])
    away = (y - (half * 2 + owner_tm)) % 4
    part = wanted
    for k in range(1, 4):
        got = lax.ppermute(wanted, ("col", "tm"), y_shift(k))
        part = jnp.where(away == k, got, part)
    line = ring_gather(part[0], "row", x_shift, row // 4)
    plane = ring_gather(line, "row", z_shift, row % 4)
    raw = plane.transpose(1, 0, 2, 3).reshape(S, PANEL)
    pivots = pair(dot_nn(whitening, raw).astype(BF16), 1)
    s0, s1 = pivots[0], pivots[1]
    own_part = jnp.where(col // 2 == 0, part[1], part[2])
    own_raw = lax.all_gather(own_part, "row", axis=0, tiled=True)
    sc = dot_nn(whitening, own_raw).astype(BF16)

    ridges = pair(pair(ridge, 1), 2).reshape(4, PANEL)
    g0 = lax.dynamic_slice_in_dim(ridges, q0, 1, 0)
    g1 = lax.dynamic_slice_in_dim(ridges, q1, 1, 0)

    moved = lax.all_to_all(local, "row", split_axis=1, concat_axis=0, tiled=True)
    series = moved.reshape(S, S)
    own = lax.dot_general(
        series, whitening, (((0,), (1,)), ((), ())), preferred_element_type=F32
    ).astype(BF16)
    far = swap(own, 2)
    xs = (own, swap(own, 1), far, swap(far, 1))

    inv0, u, inv1 = chain(s0, s1, g0, g1)

    holds = (row == owner_row) & (tm == owner_tm)
    done = (col == q0) | (col == q1)

    def slab_tile(q):
        return jnp.where(holds, half * 4 + q, -1)

    info = jnp.stack([col, slab_tile(q0), slab_tile(q1), slab_tile(col), done.astype(jnp.int32)])
    consts = (s0, s1, sc, inv0, u, inv1, g0, g1, ridge[None, :])
    return finish(info.astype(jnp.int32), xs, consts)


def solution(mesh):
    in_specs = (P("row", None, "tm", "col"), P(), P("col"), P(), P())
    out_specs = (P(("row", "tm"), "col"), P(None, ("row", "tm"), None))
    return jax.shard_map(
        on_device, mesh=mesh, in_specs=in_specs, out_specs=out_specs, check_vma=False
    )
```

```python
import jax
import jax.numpy as jnp
from jax import lax
from jax.experimental import pallas as pl
from jax.experimental.pallas import tpu as pltpu
from jax.sharding import PartitionSpec as P

S = 1024
PANEL = 512
TILE = 512
BLOCK = 128
SCALE = 1.0 / 32.0
HIGH = lax.Precision.HIGHEST
F32 = jnp.float32
BF16 = jnp.bfloat16


def place(y, core):
    return ((y // 2) * 2 + core) * 2 + y % 2


def y_shift(k):
    return [(place(y, m), place((y + k) % 4, m)) for y in range(4) for m in range(2)]


def x_shift(k):
    return [(x * 4 + z, ((x + k) % 4) * 4 + z) for x in range(4) for z in range(4)]


def z_shift(k):
    return [(x * 4 + z, x * 4 + (z + k) % 4) for x in range(4) for z in range(4)]


def swap(value, bit):
    return lax.ppermute(value, "col", [(c, c ^ bit) for c in range(4)])


def ring_gather(piece, axis, shift, own):
    full = jnp.zeros((4,) + piece.shape, piece.dtype)
    full = lax.dynamic_update_index_in_dim(full, piece, own, 0)
    for k in range(1, 4):
        got = lax.ppermute(piece, axis, shift(k))
        full = lax.dynamic_update_index_in_dim(full, got, (own - k) % 4, 0)
    return full


def dot_nn(a, b):
    return jnp.dot(a, b, preferred_element_type=F32)


def dot_tn(a, b, precision=None):
    return lax.dot_general(
        a, b, (((0,), (0,)), ((), ())), precision=precision, preferred_element_type=F32
    )


def dot_nt(a, b):
    return lax.dot_general(a, b, (((1,), (1,)), ((), ())), preferred_element_type=F32)


def halves(value):
    high = value.astype(BF16)
    return high, (value - high.astype(F32)).astype(BF16)


def thirds(value):
    high = value.astype(BF16).astype(F32)
    rest = value - high
    middle = rest.astype(BF16).astype(F32)
    return high, middle, rest - middle


def outer(rows):
    h, m, l = thirds(rows)
    w = BLOCK
    left = jnp.concatenate([h[:, :w], h[:, :w], m[:, :w], m[:, :w], h[:, :w], l[:, :w]], 0)
    right = jnp.concatenate([h, m, h, m, l, h], 0)
    return dot_tn(left.astype(BF16), right.astype(BF16))


def factor_block(w, spare):
    sub = lax.broadcasted_iota(jnp.int32, (8, BLOCK), 0)
    for k in range(0, BLOCK, 8):
        left = w[k : k + 8, :BLOCK]
        right = w[k : k + 8, BLOCK:]
        d = {}
        for j in range(8):
            column = jnp.broadcast_to(left[:, k + j : k + j + 1], (8, BLOCK))
            for i in range(j, 8):
                d[i, j] = jnp.broadcast_to(column[i : i + 1, :], (8, BLOCK))
        lefts, rights = [], []
        new_left = jnp.zeros((8, BLOCK), F32)
        new_right = jnp.zeros((8, BLOCK), F32)
        for j in range(8):
            r = lax.rsqrt(d[j, j])
            for i in range(j + 1, 8):
                d[i, j] = d[i, j] * r
            for i in range(j + 1, 8):
                for n in range(i, 8):
                    d[n, i] = d[n, i] - d[n, j] * d[i, j]
            a = jnp.broadcast_to(left[j : j + 1, :], (8, BLOCK))
            b = jnp.broadcast_to(right[j : j + 1, :], (8, BLOCK))
            for i in range(j):
                a = a - d[j, i] * lefts[i]
                b = b - d[j, i] * rights[i]
            lefts.append(a * r)
            rights.append(b * r)
            new_left = jnp.where(sub == j, lefts[j], new_left)
            new_right = jnp.where(sub == j, rights[j], new_right)
        w[k : k + 8, :BLOCK] = new_left
        w[k : k + 8, BLOCK:] = new_right
        if k + 8 < BLOCK:
            update = outer(jnp.concatenate([new_left, new_right], 1))
            w[k + 8 :, :] = w[k + 8 :, :] - update[k + 8 :, :]
        if spare and k % 32 == 0:
            spare.pop(0)()


def eye(n):
    return lax.broadcasted_iota(jnp.int32, (n, n), 0) == lax.broadcasted_iota(jnp.int32, (n, n), 1)


def eliminate(m, w, spare):
    extra = m.shape[1] - PANEL
    for r0 in range(0, PANEL, BLOCK):
        r1 = r0 + BLOCK
        w[:, :BLOCK] = m[r0:r1, r0:r1]
        w[:, BLOCK:] = eye(BLOCK).astype(F32)
        factor_block(w, spare)
        rows = jnp.dot(w[:, BLOCK:], m[r0:r1, r1 : extra + r1], precision=HIGH)
        m[r0:r1, r1 : extra + r1] = rows
        if r1 < PANEL:
            m[r1:, r1 : extra + r1] -= dot_tn(rows[:, : PANEL - r1], rows, HIGH)


def chain0_kernel(s0, s1, g0, inv0, u, m0, w):
    unit = eye(PANEL)
    m0[:, :PANEL] = dot_tn(s0[...], s0[...]) * SCALE + jnp.where(unit, g0[...], 0.0)
    m0[:, PANEL : 2 * PANEL] = dot_tn(s0[...], s1[...]) * SCALE
    m0[:, 2 * PANEL :] = unit.astype(F32)
    eliminate(m0, w, [])
    inv0[...] = m0[:, 2 * PANEL :]
    u[...] = m0[:, PANEL : 2 * PANEL].astype(BF16)


def chain0(s0, s1, g0):
    vmem = pl.BlockSpec(memory_space=pltpu.VMEM)
    return pl.pallas_call(
        chain0_kernel,
        out_shape=(
            jax.ShapeDtypeStruct((PANEL, PANEL), F32),
            jax.ShapeDtypeStruct((PANEL, PANEL), BF16),
        ),
        in_specs=[vmem] * 3,
        out_specs=(vmem, vmem),
        scratch_shapes=[pltpu.VMEM((PANEL, 3 * PANEL), F32), pltpu.VMEM((BLOCK, 2 * BLOCK), F32)],
        compiler_params=pltpu.CompilerParams(vmem_limit_bytes=24 << 20),
        cost_estimate=pl.CostEstimate(flops=10**9, transcendentals=0, bytes_accessed=5 << 20),
        name="chain0",
    )(s0, s1, g0)


def chain1_kernel(s0, s1, sc, g1, inv0, u, inv1, w0, w1, v, f0, f1, m1, e1, w):
    unit = eye(PANEL)
    pivot = dot_tn(s1[...], s1[...]) * SCALE + jnp.where(unit, g1[...], 0.0)
    m1[:, :PANEL] = pivot - dot_tn(u[...], u[...])
    m1[:, PANEL:] = unit.astype(F32)
    h0, l0 = halves(inv0[...])
    spare = []

    def product(at):
        def run():
            rows = s0[at : at + BLOCK, :]
            w0[at : at + BLOCK, :] = (dot_nt(rows, h0) + dot_nt(rows, l0)).astype(BF16)
        return run

    def coupling(at):
        def run():
            part = sc[:, at : at + BLOCK]
            eh, el = halves(dot_tn(s0[...], part) * SCALE)
            c0 = (dot_nn(h0, eh) + dot_nn(h0, el) + dot_nn(l0, eh)).astype(BF16)
            f0[:, at : at + BLOCK] = c0
            e1[:, at : at + BLOCK] = dot_tn(s1[...], part) * SCALE - dot_tn(u[...], c0)
        return run

    spare = [product(at) for at in range(0, S, BLOCK)]
    spare += [coupling(at) for at in range(0, PANEL, BLOCK)]
    eliminate(m1, w, spare)
    inv1[...] = m1[:, PANEL:]
    h1, l1 = halves(inv1[...])
    w1[...] = (dot_nt(s1[...], h1) + dot_nt(s1[...], l1)).astype(BF16)
    v[...] = (dot_nt(u[...], h1) + dot_nt(u[...], l1)).astype(BF16)
    eh, el = halves(e1[...])
    f1[...] = (dot_nn(h1, eh) + dot_nn(h1, el) + dot_nn(l1, eh)).astype(BF16)


def chain1(s0, s1, sc, g1, inv0, u):
    vmem = pl.BlockSpec(memory_space=pltpu.VMEM)
    small = jax.ShapeDtypeStruct((PANEL, PANEL), BF16)
    tall = jax.ShapeDtypeStruct((S, PANEL), BF16)
    return pl.pallas_call(
        chain1_kernel,
        out_shape=(jax.ShapeDtypeStruct((PANEL, PANEL), F32), tall, tall, small, small, small),
        in_specs=[vmem] * 6,
        out_specs=(vmem,) * 6,
        scratch_shapes=[
            pltpu.VMEM((PANEL, 2 * PANEL), F32),
            pltpu.VMEM((PANEL, PANEL), F32),
            pltpu.VMEM((BLOCK, 2 * BLOCK), F32),
        ],
        compiler_params=pltpu.CompilerParams(vmem_limit_bytes=28 << 20),
        cost_estimate=pl.CostEstimate(flops=35 * 10**9, transcendentals=0, bytes_accessed=8 << 20),
        name="chain1",
    )(s0, s1, sc, g1, inv0, u)


def finish_kernel(
    info, own, near, far0, far1, next0, next1, w0, w1, v, sc, f0, f1, inv0, inv1, g0, g1, gc,
    t_ref, f_ref, x, sems,
):
    i = pl.program_id(0)
    tiles = [own.at[:TILE], own.at[TILE:], near.at[:TILE], near.at[TILE:], far0, far1, next0, next1]

    def fetch(m):
        return pltpu.make_async_copy(tiles[m], x.at[m % 2], sems.at[m % 2])

    for m in range(8):
        @pl.when(i == m)
        def _(m=m):
            if m == 0:
                fetch(0).start()
            if m < 7:
                fetch(m + 1).start()
            fetch(m).wait()

    tile = (info[0] ^ (i // 2)) * 2 + i % 2
    xs = x[i % 2]

    f_ref[0] = (dot_nn(xs, w0[...]) * SCALE).astype(BF16)

    @pl.when(tile == info[1])
    def _():
        ridge = jnp.where(eye(PANEL), g0[...], 0.0)
        add = lax.dot_general(ridge, inv0[...], (((1,), (1,)), ((), ())), precision=HIGH)
        f_ref[0] = (dot_nn(xs, w0[...]) * SCALE + add).astype(BF16)

    p0 = f_ref[0]
    f_ref[1] = (dot_nn(xs, w1[...]) * SCALE - dot_nn(p0, v[...])).astype(BF16)

    @pl.when(tile == info[2])
    def _():
        ridge = jnp.where(eye(PANEL), g1[...], 0.0)
        add = lax.dot_general(ridge, inv1[...], (((1,), (1,)), ((), ())), precision=HIGH)
        f_ref[1] = (dot_nn(xs, w1[...]) * SCALE - dot_nn(p0, v[...]) + add).astype(BF16)

    @pl.when(info[4] == 1)
    def _():
        t_ref[...] = jnp.zeros_like(t_ref)

    @pl.when(info[4] == 0)
    def _():
        on = (tile == info[3]).astype(F32)
        add = jnp.where(eye(PANEL), on * gc[...], 0.0)
        t_ref[...] = (
            dot_nn(xs, sc[...]) * SCALE + add - dot_nn(p0, f0[...]) - dot_nn(f_ref[1], f1[...])
        )


def finish(info, xs, consts):
    def tile(i, info):
        return (info[0] ^ (i // 2)) * 2 + i % 2

    hbm = pl.BlockSpec(memory_space=pl.ANY)
    vmem = pl.BlockSpec(memory_space=pltpu.VMEM)
    return pl.pallas_call(
        finish_kernel,
        out_shape=(
            jax.ShapeDtypeStruct((4 * S, PANEL), F32),
            jax.ShapeDtypeStruct((2, 4 * S, PANEL), BF16),
        ),
        grid_spec=pltpu.PrefetchScalarGridSpec(
            num_scalar_prefetch=1,
            grid=(8,),
            in_specs=[hbm] * len(xs) + [vmem] * len(consts),
            out_specs=(
                pl.BlockSpec((TILE, PANEL), lambda i, info: (tile(i, info), 0)),
                pl.BlockSpec((2, TILE, PANEL), lambda i, info: (0, tile(i, info), 0)),
            ),
            scratch_shapes=[pltpu.VMEM((2, TILE, S), BF16), pltpu.SemaphoreType.DMA((2,))],
        ),
        compiler_params=pltpu.CompilerParams(vmem_limit_bytes=28 << 20),
        name="finish",
    )(info, *xs, *consts)


def on_device(samples, whitening, ridge, slab_start, panels):
    col = lax.axis_index("col")
    tm = lax.axis_index("tm")
    row = lax.axis_index("row")
    core = col % 2
    y = (col // 2) * 2 + tm
    slab = slab_start[0]
    half, owner_tm, owner_row = slab % 2, (slab // 2) % 2, slab // 4
    q0, q1 = panels[0], panels[1]
    local = samples[:, :, 0, :]

    def pair(value, bit):
        other = swap(value, bit)
        upper = (col & bit) != 0
        return jnp.stack([jnp.where(upper, other, value), jnp.where(upper, value, other)])

    mine = lax.dynamic_index_in_dim(local, owner_row, 1, keepdims=False)
    chip = pair(mine, 1)

    def panel_of(values, q):
        start = (q // 2, 0, (q % 2) * PANEL)
        return lax.dynamic_slice(values, start, (1, values.shape[1], PANEL))[0]

    wanted = jnp.stack([panel_of(chip, jnp.where(core == 0, q0, q1)), panel_of(chip, core), panel_of(chip, core + 2)])
    away = (y - (half * 2 + owner_tm)) % 4
    part = wanted
    for k in range(1, 4):
        got = lax.ppermute(wanted, ("col", "tm"), y_shift(k))
        part = jnp.where(away == k, got, part)
    ridges = pair(pair(ridge, 1), 2).reshape(4, PANEL)
    part, ridges, local = lax.optimization_barrier((part, ridges, local))
    g0 = lax.dynamic_slice_in_dim(ridges, q0, 1, 0)
    g1 = lax.dynamic_slice_in_dim(ridges, q1, 1, 0)
    crossed = swap(local[:, :, :PANEL], 2)
    own_part = jnp.where(col // 2 == 0, part[1], part[2])
    own_raw = lax.all_gather(own_part, "row", axis=0, tiled=True)
    line = ring_gather(part[0], "row", x_shift, row // 4)
    pieces = [lax.ppermute(line, "row", z_shift(k)) for k in range(1, 4)]
    pieces[0], local = lax.optimization_barrier((pieces[0], local))
    plane = jnp.zeros((4,) + line.shape, line.dtype)
    for k, piece in enumerate([line] + pieces):
        plane = lax.dynamic_update_index_in_dim(plane, piece, (row - k) % 4, 0)
    raw = plane.transpose(1, 0, 2, 3).reshape(S, PANEL)
    pivots = pair(dot_nn(whitening, raw).astype(BF16), 1)
    s0, s1 = pivots[0], pivots[1]

    def whitened(moved):
        series = moved.reshape(S, moved.shape[-1])
        return lax.dot_general(
            series, whitening, (((0,), (1,)), ((), ())), preferred_element_type=F32
        ).astype(BF16)

    moved = lax.all_to_all(local, "row", split_axis=1, concat_axis=0, tiled=True)
    crossed, moved = lax.optimization_barrier((crossed, moved))
    moved_far = lax.all_to_all(crossed, "row", split_axis=1, concat_axis=0, tiled=True)

    inv0, u = chain0(s0, s1, g0)
    own = whitened(moved)
    own, inv0, u = lax.optimization_barrier((own, inv0, u))
    sc = dot_nn(whitening, lax.optimization_barrier((own_raw, own))[0]).astype(BF16)
    far1 = swap(own[PANEL:], 2)
    near = swap(own, 1)
    next1 = swap(far1, 1)
    inv1, w0, w1, v, f0, f1 = chain1(s0, s1, sc, g1, inv0, u)
    moved_far, w1 = lax.optimization_barrier((moved_far, w1))
    far0 = whitened(moved_far)
    xs = (own, near, far0, far1, swap(far0, 1), next1)

    holds = (row == owner_row) & (tm == owner_tm)
    done = (col == q0) | (col == q1)

    def slab_tile(q):
        return jnp.where(holds, half * 4 + q, -1)

    info = jnp.stack([col, slab_tile(q0), slab_tile(q1), slab_tile(col), done.astype(jnp.int32)])
    consts = (w0, w1, v, sc, f0, f1, inv0, inv1, g0, g1, ridge[None, :])
    return finish(info.astype(jnp.int32), xs, consts)


def solution(mesh):
    in_specs = (P("row", None, "tm", "col"), P(), P("col"), P(), P())
    out_specs = (P(("row", "tm"), "col"), P(None, ("row", "tm"), None))
    return jax.shard_map(
        on_device, mesh=mesh, in_specs=in_specs, out_specs=out_specs, check_vma=False
    )
```

```python
import jax
import jax.numpy as jnp
from jax import lax
from jax.experimental import pallas as pl
from jax.experimental.pallas import tpu as pltpu
from jax.sharding import PartitionSpec as P

S = 1024
PANEL = 512
TILE = 512
BLOCK = 128
SCALE = 1.0 / 32.0
HIGH = lax.Precision.HIGHEST
F32 = jnp.float32
BF16 = jnp.bfloat16


def place(y, core):
    return ((y // 2) * 2 + core) * 2 + y % 2


def y_shift(k):
    return [(place(y, m), place((y + k) % 4, m)) for y in range(4) for m in range(2)]


def x_shift(k):
    return [(x * 4 + z, ((x + k) % 4) * 4 + z) for x in range(4) for z in range(4)]


def z_shift(k):
    return [(x * 4 + z, x * 4 + (z + k) % 4) for x in range(4) for z in range(4)]


def swap(value, bit):
    return lax.ppermute(value, "col", [(c, c ^ bit) for c in range(4)])


def ring_gather(piece, axis, shift, own):
    full = jnp.zeros((4,) + piece.shape, piece.dtype)
    full = lax.dynamic_update_index_in_dim(full, piece, own, 0)
    for k in range(1, 4):
        got = lax.ppermute(piece, axis, shift(k))
        full = lax.dynamic_update_index_in_dim(full, got, (own - k) % 4, 0)
    return full


def dot_nn(a, b):
    return jnp.dot(a, b, preferred_element_type=F32)


def dot_tn(a, b, precision=None):
    return lax.dot_general(
        a, b, (((0,), (0,)), ((), ())), precision=precision, preferred_element_type=F32
    )


def dot_nt(a, b):
    return lax.dot_general(a, b, (((1,), (1,)), ((), ())), preferred_element_type=F32)


def halves(value):
    high = value.astype(BF16)
    return high, (value - high.astype(F32)).astype(BF16)


def thirds(value):
    high = value.astype(BF16).astype(F32)
    rest = value - high
    middle = rest.astype(BF16).astype(F32)
    return high, middle, rest - middle


def outer(rows):
    h, m, l = thirds(rows)
    w = BLOCK
    left = jnp.concatenate([h[:, :w], h[:, :w], m[:, :w], m[:, :w], h[:, :w], l[:, :w]], 0)
    right = jnp.concatenate([h, m, h, m, l, h], 0)
    return dot_tn(left.astype(BF16), right.astype(BF16))


def factor_block(w, spare):
    sub = lax.broadcasted_iota(jnp.int32, (8, BLOCK), 0)
    lane = lax.broadcasted_iota(jnp.int32, (8, BLOCK), 1)
    left, right = w[:8, :BLOCK], w[:8, BLOCK:]
    for k in range(0, BLOCK, 8):
        d = {}
        for j in range(8):
            column = jnp.broadcast_to(left[:, k + j : k + j + 1], (8, BLOCK))
            for i in range(j, 8):
                d[i, j] = jnp.broadcast_to(column[i : i + 1, :], (8, BLOCK))
        lefts, rights = [], []
        for j in range(8):
            r = lax.rsqrt(d[j, j])
            for i in range(j + 1, 8):
                d[i, j] = d[i, j] * r
            for i in range(j + 1, 8):
                for n in range(i, 8):
                    d[n, i] = d[n, i] - d[n, j] * d[i, j]
            a = jnp.broadcast_to(left[j : j + 1, :], (8, BLOCK))
            b = jnp.broadcast_to(right[j : j + 1, :], (8, BLOCK))
            for i in range(j):
                a = a - d[j, i] * lefts[i]
                b = b - d[j, i] * rights[i]
            lefts.append(a * r)
            rights.append(b * r)
        new_left = jnp.zeros((8, BLOCK), F32)
        new_right = jnp.zeros((8, BLOCK), F32)
        for j in range(8):
            new_left = jnp.where(sub == j, lefts[j], new_left)
            new_right = jnp.where(sub == j, rights[j], new_right)
        n = k + 8
        if n < BLOCK:
            left, right = w[n : n + 8, :BLOCK], w[n : n + 8, BLOCK:]
            at = lane == sub + n
            for j in range(8):
                c = jnp.sum(jnp.where(at, lefts[j], 0.0), axis=1, keepdims=True)
                left = left - c * lefts[j]
                right = right - c * rights[j]
        w[k:n, :BLOCK] = new_left
        w[k:n, BLOCK:] = new_right
        if n + 8 < BLOCK:
            update = outer(jnp.concatenate([new_left, new_right], 1))
            w[n + 8 :, :] = w[n + 8 :, :] - update[n + 8 :, :]
        if spare and k % 32 == 0:
            spare.pop(0)()


def eye(n):
    return lax.broadcasted_iota(jnp.int32, (n, n), 0) == lax.broadcasted_iota(jnp.int32, (n, n), 1)


def eliminate(m, w, spare):
    extra = m.shape[1] - PANEL
    for r0 in range(0, PANEL, BLOCK):
        r1 = r0 + BLOCK
        w[:, :BLOCK] = m[r0:r1, r0:r1]
        w[:, BLOCK:] = eye(BLOCK).astype(F32)
        factor_block(w, spare)
        rows = jnp.dot(w[:, BLOCK:], m[r0:r1, r1 : extra + r1], precision=HIGH)
        m[r0:r1, r1 : extra + r1] = rows
        if r1 < PANEL:
            m[r1:, r1 : extra + r1] -= dot_tn(rows[:, : PANEL - r1], rows, HIGH)


def copies(pairs, sems):
    return [pltpu.make_async_copy(a, b, sems.at[k]) for k, (a, b) in enumerate(pairs)]


def in_hbm(values):
    return [pltpu.with_memory_space_constraint(value, pltpu.HBM) for value in values]


def start(transfers):
    for transfer in transfers:
        transfer.start()


def wait(transfers):
    for transfer in transfers:
        transfer.wait()


def chain0_kernel(
    g0, s0_at, s1_at, inv0_at, u_at, r0_at, m0, w, s0, s1, inv0, u, r0, ins, outs
):
    fetches = copies([(s0_at, s0), (s1_at, s1)], ins)
    start(fetches)
    unit = eye(PANEL)
    m0[:, 2 * PANEL :] = unit.astype(F32)
    wait(fetches[:1])
    m0[:, :PANEL] = dot_tn(s0[...], s0[...]) * SCALE + jnp.where(unit, g0[...], 0.0)
    wait(fetches[1:])
    m0[:, PANEL : 2 * PANEL] = dot_tn(s0[...], s1[...]) * SCALE
    eliminate(m0, w, [])
    inv0[...] = m0[:, 2 * PANEL :]
    u[...] = m0[:, PANEL : 2 * PANEL].astype(BF16)
    r0[...] = (m0[:, 2 * PANEL :] * g0[...]).T
    stores = copies([(inv0, inv0_at), (u, u_at), (r0, r0_at)], outs)
    start(stores)
    wait(stores)


def chain0(s0, s1, g0):
    hbm = pl.BlockSpec(memory_space=pltpu.HBM)
    square = pltpu.HBM((PANEL, PANEL), F32)
    return pl.pallas_call(
        chain0_kernel,
        out_shape=(square, pltpu.HBM((PANEL, PANEL), BF16), square),
        in_specs=[pl.BlockSpec(memory_space=pltpu.VMEM), hbm, hbm],
        out_specs=[hbm] * 3,
        scratch_shapes=[
            pltpu.VMEM((PANEL, 3 * PANEL), F32),
            pltpu.VMEM((BLOCK, 2 * BLOCK), F32),
            pltpu.VMEM((S, PANEL), BF16),
            pltpu.VMEM((S, PANEL), BF16),
            pltpu.VMEM((PANEL, PANEL), F32),
            pltpu.VMEM((PANEL, PANEL), BF16),
            pltpu.VMEM((PANEL, PANEL), F32),
            pltpu.SemaphoreType.DMA((2,)),
            pltpu.SemaphoreType.DMA((3,)),
        ],
        compiler_params=pltpu.CompilerParams(vmem_limit_bytes=24 << 20),
        cost_estimate=pl.CostEstimate(flops=10**9, transcendentals=0, bytes_accessed=5 << 20),
        name="chain0",
    )(g0, *in_hbm((s0, s1)))


def chain1_kernel(
    g1, s0_at, s1_at, inv0_at, u_at, raw_at, whitening_at,
    w1_at, v_at, f1_at, r1_at, w0_at, sc_at, f0_at,
    m1, e1, w, s0, s1, inv0, u, raw, whitening, w1, v, f1, r1, w0, sc, f0, ins, outs,
):
    fetches = copies(
        [(s1_at, s1), (u_at, u), (inv0_at, inv0), (whitening_at, whitening), (raw_at, raw), (s0_at, s0)],
        ins,
    )
    start(fetches)
    unit = eye(PANEL)
    m1[:, PANEL:] = unit.astype(F32)
    wait(fetches[:2])
    pivot = dot_tn(s1[...], s1[...]) * SCALE + jnp.where(unit, g1[...], 0.0)
    m1[:, :PANEL] = pivot - dot_tn(u[...], u[...])
    wait(fetches[2:])
    h0, l0 = halves(inv0[...])

    def product(at):
        def run():
            rows = s0[at : at + BLOCK, :]
            w0[at : at + BLOCK, :] = (dot_nt(rows, h0) + dot_nt(rows, l0)).astype(BF16)
        return run

    def whiten(at):
        def run():
            sc[:, at : at + BLOCK] = dot_nn(whitening[...], raw[:, at : at + BLOCK]).astype(BF16)
        return run

    def coupling(at):
        def run():
            part = sc[:, at : at + BLOCK]
            eh, el = halves(dot_tn(s0[...], part) * SCALE)
            c0 = (dot_nn(h0, eh) + dot_nn(h0, el) + dot_nn(l0, eh)).astype(BF16)
            f0[:, at : at + BLOCK] = c0
            e1[:, at : at + BLOCK] = dot_tn(s1[...], part) * SCALE - dot_tn(u[...], c0)
        return run

    spare = [whiten(at) for at in range(0, PANEL, BLOCK)]
    spare += [coupling(at) for at in range(0, PANEL, BLOCK)]
    spare += [product(at) for at in range(0, S, BLOCK)]
    eliminate(m1, w, spare)
    stores = copies(
        [(w0, w0_at), (sc, sc_at), (f0, f0_at), (w1, w1_at), (v, v_at), (f1, f1_at), (r1, r1_at)],
        outs,
    )
    start(stores[:3])
    h1, l1 = halves(m1[:, PANEL:])
    w1[...] = (dot_nt(s1[...], h1) + dot_nt(s1[...], l1)).astype(BF16)
    start(stores[3:4])
    v[...] = (dot_nt(u[...], h1) + dot_nt(u[...], l1)).astype(BF16)
    eh, el = halves(e1[...])
    f1[...] = (dot_nn(h1, eh) + dot_nn(h1, el) + dot_nn(l1, eh)).astype(BF16)
    r1[...] = (m1[:, PANEL:] * g1[...]).T
    start(stores[4:])
    wait(stores)


def chain1(s0, s1, raw, whitening, g1, inv0, u):
    hbm = pl.BlockSpec(memory_space=pltpu.HBM)
    square = pltpu.HBM((PANEL, PANEL), F32)
    small = pltpu.HBM((PANEL, PANEL), BF16)
    tall = pltpu.HBM((S, PANEL), BF16)
    return pl.pallas_call(
        chain1_kernel,
        out_shape=(tall, small, small, square, tall, tall, small),
        in_specs=[pl.BlockSpec(memory_space=pltpu.VMEM)] + [hbm] * 6,
        out_specs=[hbm] * 7,
        scratch_shapes=[
            pltpu.VMEM((PANEL, 2 * PANEL), F32),
            pltpu.VMEM((PANEL, PANEL), F32),
            pltpu.VMEM((BLOCK, 2 * BLOCK), F32),
            pltpu.VMEM((S, PANEL), BF16),
            pltpu.VMEM((S, PANEL), BF16),
            pltpu.VMEM((PANEL, PANEL), F32),
            pltpu.VMEM((PANEL, PANEL), BF16),
            pltpu.VMEM((S, PANEL), BF16),
            pltpu.VMEM((S, S), BF16),
            pltpu.VMEM((S, PANEL), BF16),
            pltpu.VMEM((PANEL, PANEL), BF16),
            pltpu.VMEM((PANEL, PANEL), BF16),
            pltpu.VMEM((PANEL, PANEL), F32),
            pltpu.VMEM((S, PANEL), BF16),
            pltpu.VMEM((S, PANEL), BF16),
            pltpu.VMEM((PANEL, PANEL), BF16),
            pltpu.SemaphoreType.DMA((6,)),
            pltpu.SemaphoreType.DMA((7,)),
        ],
        compiler_params=pltpu.CompilerParams(vmem_limit_bytes=28 << 20),
        cost_estimate=pl.CostEstimate(flops=35 * 10**9, transcendentals=0, bytes_accessed=8 << 20),
        name="chain1",
    )(g1, *in_hbm((s0, s1, inv0, u, raw, whitening)))


def finish_kernel(
    info, xa, xb, gc, w0_at, w1_at, v_at, sc_at, f0_at, f1_at, r0, r1, *rest
):
    t_ref, f_ref, w0, w1, v, sc, f0, f1, add0, add1, sems, sem = rest[-12:]
    i = pl.program_id(0)
    tile = tile_of(i, info)
    consts = [(w0_at, w0), (w1_at, w1), (v_at, v), (sc_at, sc), (f0_at, f0), (f1_at, f1)]
    fetches = copies(consts, sems)

    @pl.when(i == 0)
    def _():
        start(fetches)
        wait(fetches[:3])

    for k, source, target in ((1, r0, add0), (2, r1, add1)):
        @pl.when(tile == info[k])
        def _(source=source, target=target):
            copy = pltpu.make_async_copy(source, target, sem)
            copy.start()
            copy.wait()

    xs = jnp.where(i < S // TILE, xa[...], xb[...])
    p0 = dot_nn(xs, w0[...]) * SCALE + jnp.where(tile == info[1], add0[...], 0.0)
    p0 = p0.astype(BF16)
    f_ref[0] = p0
    p1 = dot_nn(xs, w1[...]) * SCALE + jnp.where(tile == info[2], add1[...], 0.0)
    p1 = (p1 - dot_nn(p0, v[...])).astype(BF16)
    f_ref[1] = p1

    @pl.when(i == 0)
    def _():
        wait(fetches[3:])

    ridge = jnp.where(eye(PANEL) & (tile == info[3]), gc[...], 0.0)
    t = dot_nn(xs, sc[...]) * SCALE + ridge - dot_nn(p0, f0[...]) - dot_nn(p1, f1[...])
    t_ref[...] = jnp.where(info[4] == 1, 0.0, t)


def tile_of(i, info):
    half = S // TILE
    return (info[0] ^ (i // half)) * half + i % half


def finish(info, xs, gc, consts, prior=()):
    hbm = pl.BlockSpec(memory_space=pltpu.HBM)
    half = S // TILE
    at = 2 + len(xs) + len(consts)
    return pl.pallas_call(
        finish_kernel,
        out_shape=(
            jax.ShapeDtypeStruct((4 * S, PANEL), F32),
            jax.ShapeDtypeStruct((2, 4 * S, PANEL), BF16),
        ),
        grid_spec=pltpu.PrefetchScalarGridSpec(
            num_scalar_prefetch=1,
            grid=(2 * half,),
            in_specs=[
                pl.BlockSpec((TILE, S), lambda i, info: (jnp.minimum(i, half - 1), 0)),
                pl.BlockSpec((TILE, S), lambda i, info: (jnp.maximum(i - half, 0), 0)),
            ]
            + [pl.BlockSpec((1, PANEL), lambda i, info: (0, 0))]
            + [hbm] * (len(consts) + len(prior)),
            out_specs=(
                pl.BlockSpec((TILE, PANEL), lambda i, info: (tile_of(i, info), 0)),
                pl.BlockSpec((2, TILE, PANEL), lambda i, info: (0, tile_of(i, info), 0)),
            ),
            scratch_shapes=[pltpu.VMEM(value.shape, value.dtype) for value in consts]
            + [pltpu.SemaphoreType.DMA((6,)), pltpu.SemaphoreType.DMA],
        ),
        input_output_aliases={at: 0, at + 1: 1} if prior else {},
        compiler_params=pltpu.CompilerParams(vmem_limit_bytes=34 << 20),
        name="finish",
    )(info, *xs, gc, *in_hbm(consts), *prior)


def on_device(samples, whitening, ridge, slab_start, panels):
    col = lax.axis_index("col")
    tm = lax.axis_index("tm")
    row = lax.axis_index("row")
    core = col % 2
    y = (col // 2) * 2 + tm
    slab = slab_start[0]
    half, owner_tm, owner_row = slab % 2, (slab // 2) % 2, slab // 4
    q0, q1 = panels[0], panels[1]
    local = samples[:, :, 0, :]

    def pair(value, bit):
        other = swap(value, bit)
        upper = (col & bit) != 0
        return jnp.stack([jnp.where(upper, other, value), jnp.where(upper, value, other)])

    mine = lax.dynamic_index_in_dim(local, owner_row, 1, keepdims=False)
    chip = pair(mine, 1)

    def panel_of(values, q):
        start = (q // 2, 0, (q % 2) * PANEL)
        return lax.dynamic_slice(values, start, (1, values.shape[1], PANEL))[0]

    wanted = jnp.stack([panel_of(chip, jnp.where(core == 0, q0, q1)), panel_of(chip, core), panel_of(chip, core + 2)])
    wanted, local = lax.optimization_barrier((wanted, local))
    away = (y - (half * 2 + owner_tm)) % 4
    part = wanted
    for k in range(1, 4):
        got = lax.ppermute(wanted, ("col", "tm"), y_shift(k))
        part = jnp.where(away == k, got, part)
    ridges = pair(pair(ridge, 1), 2).reshape(4, PANEL)
    part, ridges = lax.optimization_barrier((part, ridges))
    g0 = lax.dynamic_slice_in_dim(ridges, q0, 1, 0)
    g1 = lax.dynamic_slice_in_dim(ridges, q1, 1, 0)
    own_part = jnp.where(col // 2 == 0, part[1], part[2])
    own_raw = lax.all_gather(own_part, "row", axis=0, tiled=True)
    line = ring_gather(part[0], "row", x_shift, row // 4)
    plane = ring_gather(line, "row", z_shift, row % 4)
    raw = plane.transpose(1, 0, 2, 3).reshape(S, PANEL)
    pivots = pair(dot_nn(whitening, raw).astype(BF16), 1)
    s0, s1 = pivots[0], pivots[1]

    moved = lax.all_to_all(local, "row", split_axis=1, concat_axis=0, tiled=True)
    moved, s0 = lax.optimization_barrier((moved, s0))
    own = lax.dot_general(
        moved.reshape(S, S), whitening, (((0,), (1,)), ((), ())), preferred_element_type=F32
    ).astype(BF16)
    far = swap(own, 2)
    own, s0 = lax.optimization_barrier((own, s0))
    inv0, u, r0 = chain0(s0, s1, g0)
    w1, v, f1, r1, w0, sc, f0 = chain1(s0, s1, own_raw, whitening, g1, inv0, u)
    far, w1 = lax.optimization_barrier((far, w1))

    holds = (row == owner_row) & (tm == owner_tm)
    done = (col == q0) | (col == q1)

    def slab_tile(q):
        return jnp.where(holds, half * 4 + q, -1)

    def info(c):
        flags = [c, slab_tile(q0), slab_tile(q1), slab_tile(col), done]
        return jnp.stack([flag.astype(jnp.int32) for flag in flags])

    consts = (w0, w1, v, sc, f0, f1, r0, r1)
    first = finish(info(col), (own, swap(own, 1)), ridge[None, :], consts)
    return finish(info(col ^ 2), (far, swap(far, 1)), ridge[None, :], consts, first)


def solution(mesh):
    in_specs = (P("row", None, "tm", "col"), P(), P("col"), P(), P())
    out_specs = (P(("row", "tm"), "col"), P(None, ("row", "tm"), None))
    return jax.shard_map(
        on_device, mesh=mesh, in_specs=in_specs, out_specs=out_specs, check_vma=False
    )
```

```python
import jax
import jax.numpy as jnp
from jax import lax
from jax.experimental import pallas as pl
from jax.experimental.pallas import tpu as pltpu
from jax.sharding import PartitionSpec as P

S = 1024
PANEL = 512
TILE = 256
BLOCK = 128
SCALE = 1.0 / 32.0
HIGH = lax.Precision.HIGHEST
F32 = jnp.float32
BF16 = jnp.bfloat16


def place(y, core):
    return ((y // 2) * 2 + core) * 2 + y % 2


def y_shift(k):
    return [(place(y, m), place((y + k) % 4, m)) for y in range(4) for m in range(2)]


def x_shift(k):
    return [(x * 4 + z, ((x + k) % 4) * 4 + z) for x in range(4) for z in range(4)]


def z_shift(k):
    return [(x * 4 + z, x * 4 + (z + k) % 4) for x in range(4) for z in range(4)]


def swap(value, bit):
    return lax.ppermute(value, "col", [(c, c ^ bit) for c in range(4)])


def ring_gather(piece, axis, shift, own):
    full = jnp.zeros((4,) + piece.shape, piece.dtype)
    full = lax.dynamic_update_index_in_dim(full, piece, own, 0)
    for k in range(1, 4):
        got = lax.ppermute(piece, axis, shift(k))
        full = lax.dynamic_update_index_in_dim(full, got, (own - k) % 4, 0)
    return full


def dot_nn(a, b):
    return jnp.dot(a, b, preferred_element_type=F32)


def dot_tn(a, b, precision=None):
    return lax.dot_general(
        a, b, (((0,), (0,)), ((), ())), precision=precision, preferred_element_type=F32
    )


def dot_nt(a, b):
    return lax.dot_general(a, b, (((1,), (1,)), ((), ())), preferred_element_type=F32)


def halves(value):
    high = value.astype(BF16)
    return high, (value - high.astype(F32)).astype(BF16)


def thirds(value):
    high = value.astype(BF16).astype(F32)
    rest = value - high
    middle = rest.astype(BF16).astype(F32)
    return high, middle, rest - middle


def outer(rows):
    h, m, l = thirds(rows)
    w = BLOCK
    left = jnp.concatenate([h[:, :w], h[:, :w], m[:, :w], m[:, :w], h[:, :w], l[:, :w]], 0)
    right = jnp.concatenate([h, m, h, m, l, h], 0)
    return dot_tn(left.astype(BF16), right.astype(BF16))


def factor_block(w, spare):
    sub = lax.broadcasted_iota(jnp.int32, (8, BLOCK), 0)
    lane = lax.broadcasted_iota(jnp.int32, (8, BLOCK), 1)
    left, right = w[:8, :BLOCK], w[:8, BLOCK:]
    for k in range(0, BLOCK, 8):
        d = {}
        for j in range(8):
            column = jnp.broadcast_to(left[:, k + j : k + j + 1], (8, BLOCK))
            for i in range(j, 8):
                d[i, j] = jnp.broadcast_to(column[i : i + 1, :], (8, BLOCK))
        lefts, rights = [], []
        for j in range(8):
            r = lax.rsqrt(d[j, j])
            for i in range(j + 1, 8):
                d[i, j] = d[i, j] * r
            for i in range(j + 1, 8):
                for n in range(i, 8):
                    d[n, i] = d[n, i] - d[n, j] * d[i, j]
            a = jnp.broadcast_to(left[j : j + 1, :], (8, BLOCK))
            b = jnp.broadcast_to(right[j : j + 1, :], (8, BLOCK))
            for i in range(j):
                a = a - d[j, i] * lefts[i]
                b = b - d[j, i] * rights[i]
            lefts.append(a * r)
            rights.append(b * r)
        new_left = jnp.zeros((8, BLOCK), F32)
        new_right = jnp.zeros((8, BLOCK), F32)
        for j in range(8):
            new_left = jnp.where(sub == j, lefts[j], new_left)
            new_right = jnp.where(sub == j, rights[j], new_right)
        n = k + 8
        if n < BLOCK:
            left, right = w[n : n + 8, :BLOCK], w[n : n + 8, BLOCK:]
            at = lane == sub + n
            for j in range(8):
                c = jnp.sum(jnp.where(at, lefts[j], 0.0), axis=1, keepdims=True)
                left = left - c * lefts[j]
                right = right - c * rights[j]
        w[k:n, :BLOCK] = new_left
        w[k:n, BLOCK:] = new_right
        if n + 8 < BLOCK:
            update = outer(jnp.concatenate([new_left, new_right], 1))
            w[n + 8 :, :] = w[n + 8 :, :] - update[n + 8 :, :]
        if spare and k % 32 == 0:
            spare.pop(0)()


def eye(n):
    return lax.broadcasted_iota(jnp.int32, (n, n), 0) == lax.broadcasted_iota(jnp.int32, (n, n), 1)


def eliminate(m, w, spare):
    extra = m.shape[1] - PANEL
    for r0 in range(0, PANEL, BLOCK):
        r1 = r0 + BLOCK
        w[:, :BLOCK] = m[r0:r1, r0:r1]
        w[:, BLOCK:] = eye(BLOCK).astype(F32)
        factor_block(w, spare)
        rows = jnp.dot(w[:, BLOCK:], m[r0:r1, r1 : extra + r1], precision=HIGH)
        m[r0:r1, r1 : extra + r1] = rows
        if r1 < PANEL:
            m[r1:, r1 : extra + r1] -= dot_tn(rows[:, : PANEL - r1], rows, HIGH)


def copies(pairs, sems):
    return [pltpu.make_async_copy(a, b, sems.at[k]) for k, (a, b) in enumerate(pairs)]


def in_hbm(values):
    return [pltpu.with_memory_space_constraint(value, pltpu.HBM) for value in values]


def start(transfers):
    for transfer in transfers:
        transfer.start()


def wait(transfers):
    for transfer in transfers:
        transfer.wait()


def fetch_pair(core, mine, other, s0, s1, sems):
    pairs = copies([(mine, s0), (other, s1)], sems), copies([(other, s0), (mine, s1)], sems)
    for k in range(2):
        @pl.when(core[0] == k)
        def _(k=k):
            start(pairs[k])
    return pairs[0]


def chain0_kernel(
    core, g0, mine_at, other_at, inv0_at, u_at, r0_at, m0, w, s0, s1, inv0, u, r0, ins, outs
):
    fetches = fetch_pair(core, mine_at, other_at, s0, s1, ins)
    unit = eye(PANEL)
    m0[:, 2 * PANEL :] = unit.astype(F32)
    wait(fetches[:1])
    m0[:, :PANEL] = dot_tn(s0[...], s0[...]) * SCALE + jnp.where(unit, g0[...], 0.0)
    wait(fetches[1:])
    m0[:, PANEL : 2 * PANEL] = dot_tn(s0[...], s1[...]) * SCALE
    eliminate(m0, w, [])
    inv0[...] = m0[:, 2 * PANEL :]
    u[...] = m0[:, PANEL : 2 * PANEL].astype(BF16)
    r0[...] = (m0[:, 2 * PANEL :] * g0[...]).T
    stores = copies([(inv0, inv0_at), (u, u_at), (r0, r0_at)], outs)
    start(stores)
    wait(stores)


def chain0(core, mine, other, g0):
    hbm = pl.BlockSpec(memory_space=pltpu.HBM)
    square = pltpu.HBM((PANEL, PANEL), F32)
    return pl.pallas_call(
        chain0_kernel,
        out_shape=(square, pltpu.HBM((PANEL, PANEL), BF16), square),
        in_specs=[
            pl.BlockSpec(memory_space=pltpu.SMEM), pl.BlockSpec(memory_space=pltpu.VMEM), hbm, hbm
        ],
        out_specs=[hbm] * 3,
        scratch_shapes=[
            pltpu.VMEM((PANEL, 3 * PANEL), F32),
            pltpu.VMEM((BLOCK, 2 * BLOCK), F32),
            pltpu.VMEM((S, PANEL), BF16),
            pltpu.VMEM((S, PANEL), BF16),
            pltpu.VMEM((PANEL, PANEL), F32),
            pltpu.VMEM((PANEL, PANEL), BF16),
            pltpu.VMEM((PANEL, PANEL), F32),
            pltpu.SemaphoreType.DMA((2,)),
            pltpu.SemaphoreType.DMA((3,)),
        ],
        compiler_params=pltpu.CompilerParams(vmem_limit_bytes=24 << 20),
        cost_estimate=pl.CostEstimate(flops=10**6, transcendentals=0, bytes_accessed=1 << 10),
        name="chain0",
    )(core, g0, *in_hbm((mine, other)))


def chain1_kernel(
    core, g1, mine_at, other_at, inv0_at, u_at, raw_at, whitening_at,
    w1_at, v_at, f1_at, r1_at, w0_at, sc_at, f0_at,
    m1, e1, w, s0, s1, inv0, u, raw, whitening, w1, v, f1, r1, w0, sc, f0, panel_ins, ins, outs,
):
    panels = fetch_pair(core, mine_at, other_at, s0, s1, panel_ins)
    fetches = copies(
        [(u_at, u), (inv0_at, inv0), (whitening_at, whitening), (raw_at, raw)], ins
    )
    start(fetches)
    unit = eye(PANEL)
    m1[:, PANEL:] = unit.astype(F32)
    wait(panels + fetches[:1])
    pivot = dot_tn(s1[...], s1[...]) * SCALE + jnp.where(unit, g1[...], 0.0)
    m1[:, :PANEL] = pivot - dot_tn(u[...], u[...])
    wait(fetches[1:])
    h0, l0 = halves(inv0[...])

    def product(at):
        def run():
            rows = s0[at : at + BLOCK, :]
            w0[at : at + BLOCK, :] = (dot_nt(rows, h0) + dot_nt(rows, l0)).astype(BF16)
        return run

    def whiten(at):
        def run():
            sc[:, at : at + BLOCK] = dot_nn(whitening[...], raw[:, at : at + BLOCK]).astype(BF16)
        return run

    def coupling(at):
        def run():
            part = sc[:, at : at + BLOCK]
            eh, el = halves(dot_tn(s0[...], part) * SCALE)
            c0 = (dot_nn(h0, eh) + dot_nn(h0, el) + dot_nn(l0, eh)).astype(BF16)
            f0[:, at : at + BLOCK] = c0
            e1[:, at : at + BLOCK] = dot_tn(s1[...], part) * SCALE - dot_tn(u[...], c0)
        return run

    spare = [whiten(at) for at in range(0, PANEL, BLOCK)]
    spare += [coupling(at) for at in range(0, PANEL, BLOCK)]
    spare += [product(at) for at in range(0, S, BLOCK)]
    eliminate(m1, w, spare)
    stores = copies(
        [(w0, w0_at), (sc, sc_at), (f0, f0_at), (w1, w1_at), (v, v_at), (f1, f1_at), (r1, r1_at)],
        outs,
    )
    start(stores[:3])
    h1, l1 = halves(m1[:, PANEL:])
    w1[...] = (dot_nt(s1[...], h1) + dot_nt(s1[...], l1)).astype(BF16)
    start(stores[3:4])
    v[...] = (dot_nt(u[...], h1) + dot_nt(u[...], l1)).astype(BF16)
    eh, el = halves(e1[...])
    f1[...] = (dot_nn(h1, eh) + dot_nn(h1, el) + dot_nn(l1, eh)).astype(BF16)
    r1[...] = (m1[:, PANEL:] * g1[...]).T
    start(stores[4:])
    wait(stores)


def chain1(core, mine, other, raw, whitening, g1, inv0, u):
    hbm = pl.BlockSpec(memory_space=pltpu.HBM)
    square = pltpu.HBM((PANEL, PANEL), F32)
    small = pltpu.HBM((PANEL, PANEL), BF16)
    tall = pltpu.HBM((S, PANEL), BF16)
    return pl.pallas_call(
        chain1_kernel,
        out_shape=(tall, small, small, square, tall, tall, small),
        in_specs=[pl.BlockSpec(memory_space=pltpu.SMEM), pl.BlockSpec(memory_space=pltpu.VMEM)]
        + [hbm] * 6,
        out_specs=[hbm] * 7,
        scratch_shapes=[
            pltpu.VMEM((PANEL, 2 * PANEL), F32),
            pltpu.VMEM((PANEL, PANEL), F32),
            pltpu.VMEM((BLOCK, 2 * BLOCK), F32),
            pltpu.VMEM((S, PANEL), BF16),
            pltpu.VMEM((S, PANEL), BF16),
            pltpu.VMEM((PANEL, PANEL), F32),
            pltpu.VMEM((PANEL, PANEL), BF16),
            pltpu.VMEM((S, PANEL), BF16),
            pltpu.VMEM((S, S), BF16),
            pltpu.VMEM((S, PANEL), BF16),
            pltpu.VMEM((PANEL, PANEL), BF16),
            pltpu.VMEM((PANEL, PANEL), BF16),
            pltpu.VMEM((PANEL, PANEL), F32),
            pltpu.VMEM((S, PANEL), BF16),
            pltpu.VMEM((S, PANEL), BF16),
            pltpu.VMEM((PANEL, PANEL), BF16),
            pltpu.SemaphoreType.DMA((2,)),
            pltpu.SemaphoreType.DMA((4,)),
            pltpu.SemaphoreType.DMA((7,)),
        ],
        compiler_params=pltpu.CompilerParams(vmem_limit_bytes=28 << 20),
        cost_estimate=pl.CostEstimate(flops=35 * 10**9, transcendentals=0, bytes_accessed=8 << 20),
        name="chain1",
    )(core, g1, *in_hbm((mine, other, inv0, u, raw, whitening)))


def finish_kernel(
    info, xa, xb, gc, w0_at, w1_at, v_at, sc_at, f0_at, f1_at, r0, r1, *rest
):
    t_ref, f_ref, w0, w1, v, sc, f0, f1, add0, add1, sems, sem = rest[-12:]
    i = pl.program_id(0)
    tile = tile_of(i, info)
    panel = tile // (PANEL // TILE)
    inside = tile % (PANEL // TILE) * TILE
    consts = [(w0_at, w0), (w1_at, w1), (v_at, v), (sc_at, sc), (f0_at, f0), (f1_at, f1)]
    fetches = copies(consts, sems)

    @pl.when(i == 0)
    def _():
        start(fetches)

    for k, source, target in ((1, r0, add0), (2, r1, add1)):
        @pl.when(panel == info[k])
        def _(source=source, target=target):
            copy = pltpu.make_async_copy(source.at[pl.ds(inside, TILE)], target, sem)
            copy.start()
            copy.wait()

    @pl.when(i == 0)
    def _():
        wait(fetches[:1])

    xs = jnp.where(i < pl.num_programs(0) // 2, xa[...], xb[...])
    p0 = dot_nn(xs, w0[...]) * SCALE + jnp.where(panel == info[1], add0[...], 0.0)
    p0 = p0.astype(BF16)
    f_ref[0] = p0

    @pl.when(i == 0)
    def _():
        wait(fetches[1:])

    p1 = dot_nn(xs, w1[...]) * SCALE + jnp.where(panel == info[2], add1[...], 0.0)
    p1 = (p1 - dot_nn(p0, v[...])).astype(BF16)
    f_ref[1] = p1
    row = lax.broadcasted_iota(jnp.int32, (TILE, PANEL), 0) + inside
    diagonal = row == lax.broadcasted_iota(jnp.int32, (TILE, PANEL), 1)
    ridge = jnp.where(diagonal & (panel == info[3]), gc[...], 0.0)
    t = dot_nn(xs, sc[...]) * SCALE + ridge - dot_nn(p0, f0[...]) - dot_nn(p1, f1[...])
    t_ref[...] = jnp.where(info[4] == 1, 0.0, t)


def tile_of(i, info):
    each = pl.num_programs(0) // 2
    return (info[0] ^ (i // each)) * (S // TILE) + info[5] + i % each


def finish(info, xs, gc, consts, prior=()):
    hbm = pl.BlockSpec(memory_space=pl.ANY)
    each = xs[0].shape[0] // TILE
    at = 2 + len(xs) + len(consts)

    def tile(i, info):
        return (info[0] ^ (i // each)) * (S // TILE) + info[5] + i % each

    return pl.pallas_call(
        finish_kernel,
        out_shape=(
            jax.ShapeDtypeStruct((4 * S, PANEL), F32),
            jax.ShapeDtypeStruct((2, 4 * S, PANEL), BF16),
        ),
        grid_spec=pltpu.PrefetchScalarGridSpec(
            num_scalar_prefetch=1,
            grid=(2 * each,),
            in_specs=[
                pl.BlockSpec((TILE, S), lambda i, info: (jnp.minimum(i, each - 1), 0)),
                pl.BlockSpec((TILE, S), lambda i, info: (jnp.maximum(i - each, 0), 0)),
            ]
            + [pl.BlockSpec((1, PANEL), lambda i, info: (0, 0))]
            + [hbm] * (len(consts) + len(prior)),
            out_specs=(
                pl.BlockSpec((TILE, PANEL), lambda i, info: (tile(i, info), 0)),
                pl.BlockSpec((2, TILE, PANEL), lambda i, info: (0, tile(i, info), 0)),
            ),
            scratch_shapes=[pltpu.VMEM(value.shape, value.dtype) for value in consts[:6]]
            + [pltpu.VMEM((TILE, PANEL), F32), pltpu.VMEM((TILE, PANEL), F32)]
            + [pltpu.SemaphoreType.DMA((6,)), pltpu.SemaphoreType.DMA],
        ),
        input_output_aliases={at: 0, at + 1: 1} if prior else {},
        compiler_params=pltpu.CompilerParams(vmem_limit_bytes=34 << 20),
        name="finish",
    )(info, *xs, gc, *in_hbm(consts), *prior)


def on_device(samples, whitening, ridge, slab_start, panels):
    col = lax.axis_index("col")
    tm = lax.axis_index("tm")
    row = lax.axis_index("row")
    core = col % 2
    y = (col // 2) * 2 + tm
    slab = slab_start[0]
    half, owner_tm, owner_row = slab % 2, (slab // 2) % 2, slab // 4
    q0, q1 = panels[0], panels[1]
    local = samples[:, :, 0, :]

    def pair(value, bit):
        other = swap(value, bit)
        upper = (col & bit) != 0
        return jnp.stack([jnp.where(upper, other, value), jnp.where(upper, value, other)])

    mine = lax.dynamic_index_in_dim(local, owner_row, 1, keepdims=False)
    chip = pair(mine, 1)

    def panel_of(values, q):
        start = (q // 2, 0, (q % 2) * PANEL)
        return lax.dynamic_slice(values, start, (1, values.shape[1], PANEL))[0]

    wanted = jnp.stack([panel_of(chip, jnp.where(core == 0, q0, q1)), panel_of(chip, core), panel_of(chip, core + 2)])
    away = (y - (half * 2 + owner_tm)) % 4
    part = wanted
    for k in range(1, 4):
        got = lax.ppermute(wanted, ("col", "tm"), y_shift(k))
        part = jnp.where(away == k, got, part)
    own_part = jnp.where(col // 2 == 0, part[1], part[2])
    own_raw = lax.all_gather(own_part, "row", axis=0, tiled=True)
    line = ring_gather(part[0], "row", z_shift, row % 4).reshape(S // 4, PANEL)
    line, ridge_sent = lax.optimization_barrier((line, ridge))
    pieces = [line] + [lax.ppermute(line, "row", x_shift(k)) for k in range(1, 4)]
    ridges = pair(pair(ridge_sent, 1), 2).reshape(4, PANEL)
    g0 = lax.dynamic_slice_in_dim(ridges, q0, 1, 0)
    g1 = lax.dynamic_slice_in_dim(ridges, q1, 1, 0)
    pieces[1], local = lax.optimization_barrier((pieces[1], local))
    total = 0.0
    for k, piece in enumerate(pieces):
        columns = (row // 4 - k) % 4 * (S // 4)
        total = total + dot_nn(lax.dynamic_slice_in_dim(whitening, columns, S // 4, 1), piece)
    pivot = total.astype(BF16)
    other = swap(pivot, 1)

    moved = lax.all_to_all(local, "row", split_axis=1, concat_axis=0, tiled=True)
    which = core.astype(jnp.int32)[None]
    inv0, u, r0 = chain0(which, pivot, other, g0)
    moved, own_raw, inv0, u = lax.optimization_barrier((moved, own_raw, inv0, u))
    own = lax.dot_general(
        moved.reshape(S, S), whitening, (((0,), (1,)), ((), ())), preferred_element_type=F32
    ).astype(BF16)
    far0, far1 = swap(own[:PANEL], 2), swap(own[PANEL:], 2)
    near = swap(own, 1)
    own, u = lax.optimization_barrier((own, u))
    w1, v, f1, r1, w0, sc, f0 = chain1(which, pivot, other, own_raw, whitening, g1, inv0, u)
    far0, w1 = lax.optimization_barrier((far0, w1))

    holds = (row == owner_row) & (tm == owner_tm)
    done = (col == q0) | (col == q1)

    def slab_tile(q):
        return jnp.where(holds, half * 4 + q, -1)

    def info(c, tile):
        flags = [c, slab_tile(q0), slab_tile(q1), slab_tile(col), done, jnp.int32(tile)]
        return jnp.stack([flag.astype(jnp.int32) for flag in flags])

    consts = (w0, w1, v, sc, f0, f1, r0, r1)
    gc = ridge[None, :]
    out = finish(info(col, 0), (own, near), gc, consts)
    far1, out = lax.optimization_barrier((far1, out))
    out = finish(info(col ^ 2, 0), (far0, swap(far0, 1)), gc, consts, out)
    return finish(info(col ^ 2, PANEL // TILE), (far1, swap(far1, 1)), gc, consts, out)


def solution(mesh):
    in_specs = (P("row", None, "tm", "col"), P(), P("col"), P(), P())
    out_specs = (P(("row", "tm"), "col"), P(None, ("row", "tm"), None))
    return jax.shard_map(
        on_device, mesh=mesh, in_specs=in_specs, out_specs=out_specs, check_vma=False
    )
```

```python
import jax
import jax.numpy as jnp
from jax import lax
from jax.experimental import pallas as pl
from jax.experimental.pallas import tpu as pltpu
from jax.sharding import PartitionSpec as P

S = 1024
PANEL = 512
TILE = 512
BLOCK = 128
SCALE = 1.0 / 32.0
HIGH = lax.Precision.HIGHEST
F32 = jnp.float32
BF16 = jnp.bfloat16


def place(y, core):
    return ((y // 2) * 2 + core) * 2 + y % 2


def y_shift(k):
    return [(place(y, m), place((y + k) % 4, m)) for y in range(4) for m in range(2)]


def x_shift(k):
    return [(x * 4 + z, ((x + k) % 4) * 4 + z) for x in range(4) for z in range(4)]


def z_shift(k):
    return [(x * 4 + z, x * 4 + (z + k) % 4) for x in range(4) for z in range(4)]


def swap(value, bit):
    return lax.ppermute(value, "col", [(c, c ^ bit) for c in range(4)])


def ring_gather(piece, axis, shift, own):
    full = jnp.zeros((4,) + piece.shape, piece.dtype)
    full = lax.dynamic_update_index_in_dim(full, piece, own, 0)
    for k in range(1, 4):
        got = lax.ppermute(piece, axis, shift(k))
        full = lax.dynamic_update_index_in_dim(full, got, (own - k) % 4, 0)
    return full


def dot_nn(a, b):
    return jnp.dot(a, b, preferred_element_type=F32)


def dot_tn(a, b, precision=None):
    return lax.dot_general(
        a, b, (((0,), (0,)), ((), ())), precision=precision, preferred_element_type=F32
    )


def dot_nt(a, b):
    return lax.dot_general(a, b, (((1,), (1,)), ((), ())), preferred_element_type=F32)


def halves(value):
    high = value.astype(BF16)
    return high, (value - high.astype(F32)).astype(BF16)


def thirds(value):
    high = value.astype(BF16).astype(F32)
    rest = value - high
    middle = rest.astype(BF16).astype(F32)
    return high, middle, rest - middle


def outer(rows):
    h, m, l = thirds(rows)
    w = BLOCK
    left = jnp.concatenate([h[:, :w], h[:, :w], m[:, :w], m[:, :w], h[:, :w], l[:, :w]], 0)
    right = jnp.concatenate([h, m, h, m, l, h], 0)
    return dot_tn(left.astype(BF16), right.astype(BF16))


def factor_block(w, spare):
    sub = lax.broadcasted_iota(jnp.int32, (8, BLOCK), 0)
    lane = lax.broadcasted_iota(jnp.int32, (8, BLOCK), 1)
    left, right = w[:8, :BLOCK], w[:8, BLOCK:]
    for k in range(0, BLOCK, 8):
        d = {}
        for j in range(8):
            column = jnp.broadcast_to(left[:, k + j : k + j + 1], (8, BLOCK))
            for i in range(j, 8):
                d[i, j] = jnp.broadcast_to(column[i : i + 1, :], (8, BLOCK))
        lefts, rights = [], []
        for j in range(8):
            r = lax.rsqrt(d[j, j])
            for i in range(j + 1, 8):
                d[i, j] = d[i, j] * r
            for i in range(j + 1, 8):
                for n in range(i, 8):
                    d[n, i] = d[n, i] - d[n, j] * d[i, j]
            a = jnp.broadcast_to(left[j : j + 1, :], (8, BLOCK))
            b = jnp.broadcast_to(right[j : j + 1, :], (8, BLOCK))
            for i in range(j):
                a = a - d[j, i] * lefts[i]
                b = b - d[j, i] * rights[i]
            lefts.append(a * r)
            rights.append(b * r)
        new_left = jnp.zeros((8, BLOCK), F32)
        new_right = jnp.zeros((8, BLOCK), F32)
        for j in range(8):
            new_left = jnp.where(sub == j, lefts[j], new_left)
            new_right = jnp.where(sub == j, rights[j], new_right)
        n = k + 8
        if n < BLOCK:
            left, right = w[n : n + 8, :BLOCK], w[n : n + 8, BLOCK:]
            at = lane == sub + n
            for j in range(8):
                c = jnp.sum(jnp.where(at, lefts[j], 0.0), axis=1, keepdims=True)
                left = left - c * lefts[j]
                right = right - c * rights[j]
        w[k:n, :BLOCK] = new_left
        w[k:n, BLOCK:] = new_right
        if n + 8 < BLOCK:
            update = outer(jnp.concatenate([new_left, new_right], 1))
            w[n + 8 :, :] = w[n + 8 :, :] - update[n + 8 :, :]
        if spare and k % 32 == 0:
            spare.pop(0)()


def eye(n):
    return lax.broadcasted_iota(jnp.int32, (n, n), 0) == lax.broadcasted_iota(jnp.int32, (n, n), 1)


def eliminate(m, w, spare):
    extra = m.shape[1] - PANEL
    for r0 in range(0, PANEL, BLOCK):
        r1 = r0 + BLOCK
        w[:, :BLOCK] = m[r0:r1, r0:r1]
        w[:, BLOCK:] = eye(BLOCK).astype(F32)
        factor_block(w, spare)
        rows = jnp.dot(w[:, BLOCK:], m[r0:r1, r1 : extra + r1], precision=HIGH)
        m[r0:r1, r1 : extra + r1] = rows
        if r1 < PANEL:
            m[r1:, r1 : extra + r1] -= dot_tn(rows[:, : PANEL - r1], rows, HIGH)


def copies(pairs, sems):
    return [pltpu.make_async_copy(a, b, sems.at[k]) for k, (a, b) in enumerate(pairs)]


def in_hbm(values):
    return [pltpu.with_memory_space_constraint(value, pltpu.HBM) for value in values]


def start(transfers):
    for transfer in transfers:
        transfer.start()


def wait(transfers):
    for transfer in transfers:
        transfer.wait()


def order_panels(core, mine, other, s0, s1):
    s0[...] = jnp.where(core[0] == 0, mine[...], other[...])
    s1[...] = jnp.where(core[0] == 0, other[...], mine[...])


def chain0_kernel(
    core, g0, mine, other, inv0_at, u_at, r0_at, m0, w, s0, s1, inv0, u, r0, outs
):
    order_panels(core, mine, other, s0, s1)
    unit = eye(PANEL)
    m0[:, 2 * PANEL :] = unit.astype(F32)
    m0[:, :PANEL] = dot_tn(s0[...], s0[...]) * SCALE + jnp.where(unit, g0[...], 0.0)
    m0[:, PANEL : 2 * PANEL] = dot_tn(s0[...], s1[...]) * SCALE
    eliminate(m0, w, [])
    inv0[...] = m0[:, 2 * PANEL :]
    u[...] = m0[:, PANEL : 2 * PANEL].astype(BF16)
    r0[...] = (m0[:, 2 * PANEL :] * g0[...]).T
    stores = copies([(inv0, inv0_at), (u, u_at), (r0, r0_at)], outs)
    start(stores)
    wait(stores)


def chain0(core, mine, other, g0):
    hbm = pl.BlockSpec(memory_space=pltpu.HBM)
    square = pltpu.HBM((PANEL, PANEL), F32)
    return pl.pallas_call(
        chain0_kernel,
        out_shape=(square, pltpu.HBM((PANEL, PANEL), BF16), square),
        in_specs=[pl.BlockSpec(memory_space=pltpu.SMEM)]
        + [pl.BlockSpec(memory_space=pltpu.VMEM)] * 3,
        out_specs=[hbm] * 3,
        scratch_shapes=[
            pltpu.VMEM((PANEL, 3 * PANEL), F32),
            pltpu.VMEM((BLOCK, 2 * BLOCK), F32),
            pltpu.VMEM((S, PANEL), BF16),
            pltpu.VMEM((S, PANEL), BF16),
            pltpu.VMEM((PANEL, PANEL), F32),
            pltpu.VMEM((PANEL, PANEL), BF16),
            pltpu.VMEM((PANEL, PANEL), F32),
            pltpu.SemaphoreType.DMA((3,)),
        ],
        compiler_params=pltpu.CompilerParams(vmem_limit_bytes=24 << 20),
        cost_estimate=pl.CostEstimate(flops=10**6, transcendentals=0, bytes_accessed=1 << 10),
        name="chain0",
    )(core, g0, mine, other)


def chain1_kernel(
    core, g1, mine, other, inv0_at, u_at, raw_at, whitening_at,
    w1_at, v_at, f1_at, r1_at, w0_at, sc_at, f0_at,
    m1, e1, w, s0, s1, inv0, u, raw, whitening, w1, v, f1, r1, w0, sc, f0, ins, outs,
):
    fetches = copies(
        [(u_at, u), (inv0_at, inv0), (whitening_at, whitening), (raw_at, raw)], ins
    )
    start(fetches)
    order_panels(core, mine, other, s0, s1)
    unit = eye(PANEL)
    m1[:, PANEL:] = unit.astype(F32)
    wait(fetches[:1])
    pivot = dot_tn(s1[...], s1[...]) * SCALE + jnp.where(unit, g1[...], 0.0)
    m1[:, :PANEL] = pivot - dot_tn(u[...], u[...])
    wait(fetches[1:])
    h0, l0 = halves(inv0[...])

    def product(at):
        def run():
            rows = s0[at : at + BLOCK, :]
            w0[at : at + BLOCK, :] = (dot_nt(rows, h0) + dot_nt(rows, l0)).astype(BF16)
        return run

    def whiten(at):
        def run():
            sc[:, at : at + BLOCK] = dot_nn(whitening[...], raw[:, at : at + BLOCK]).astype(BF16)
        return run

    def coupling(at):
        def run():
            part = sc[:, at : at + BLOCK]
            eh, el = halves(dot_tn(s0[...], part) * SCALE)
            c0 = (dot_nn(h0, eh) + dot_nn(h0, el) + dot_nn(l0, eh)).astype(BF16)
            f0[:, at : at + BLOCK] = c0
            e1[:, at : at + BLOCK] = dot_tn(s1[...], part) * SCALE - dot_tn(u[...], c0)
        return run

    spare = [whiten(at) for at in range(0, PANEL, BLOCK)]
    spare += [coupling(at) for at in range(0, PANEL, BLOCK)]
    spare += [product(at) for at in range(0, S, BLOCK)]
    eliminate(m1, w, spare)
    stores = copies(
        [(w0, w0_at), (sc, sc_at), (f0, f0_at), (w1, w1_at), (v, v_at), (f1, f1_at), (r1, r1_at)],
        outs,
    )
    start(stores[:3])
    h1, l1 = halves(m1[:, PANEL:])
    w1[...] = (dot_nt(s1[...], h1) + dot_nt(s1[...], l1)).astype(BF16)
    start(stores[3:4])
    v[...] = (dot_nt(u[...], h1) + dot_nt(u[...], l1)).astype(BF16)
    eh, el = halves(e1[...])
    f1[...] = (dot_nn(h1, eh) + dot_nn(h1, el) + dot_nn(l1, eh)).astype(BF16)
    r1[...] = (m1[:, PANEL:] * g1[...]).T
    start(stores[4:])
    wait(stores)


def chain1(core, mine, other, raw, whitening, g1, inv0, u):
    hbm = pl.BlockSpec(memory_space=pltpu.HBM)
    square = pltpu.HBM((PANEL, PANEL), F32)
    small = pltpu.HBM((PANEL, PANEL), BF16)
    tall = pltpu.HBM((S, PANEL), BF16)
    return pl.pallas_call(
        chain1_kernel,
        out_shape=(tall, small, small, square, tall, tall, small),
        in_specs=[pl.BlockSpec(memory_space=pltpu.SMEM)]
        + [pl.BlockSpec(memory_space=pltpu.VMEM)] * 3
        + [hbm] * 4,
        out_specs=[hbm] * 7,
        scratch_shapes=[
            pltpu.VMEM((PANEL, 2 * PANEL), F32),
            pltpu.VMEM((PANEL, PANEL), F32),
            pltpu.VMEM((BLOCK, 2 * BLOCK), F32),
            pltpu.VMEM((S, PANEL), BF16),
            pltpu.VMEM((S, PANEL), BF16),
            pltpu.VMEM((PANEL, PANEL), F32),
            pltpu.VMEM((PANEL, PANEL), BF16),
            pltpu.VMEM((S, PANEL), BF16),
            pltpu.VMEM((S, S), BF16),
            pltpu.VMEM((S, PANEL), BF16),
            pltpu.VMEM((PANEL, PANEL), BF16),
            pltpu.VMEM((PANEL, PANEL), BF16),
            pltpu.VMEM((PANEL, PANEL), F32),
            pltpu.VMEM((S, PANEL), BF16),
            pltpu.VMEM((S, PANEL), BF16),
            pltpu.VMEM((PANEL, PANEL), BF16),
            pltpu.SemaphoreType.DMA((4,)),
            pltpu.SemaphoreType.DMA((7,)),
        ],
        compiler_params=pltpu.CompilerParams(vmem_limit_bytes=28 << 20),
        cost_estimate=pl.CostEstimate(flops=35 * 10**9, transcendentals=0, bytes_accessed=8 << 20),
        name="chain1",
    )(core, g1, mine, other, *in_hbm((inv0, u, raw, whitening)))


def finish_kernel(
    info, xa, xb, gc, w0_at, w1_at, v_at, sc_at, f0_at, f1_at, r0, r1, *rest
):
    t_ref, f_ref, w0, w1, v, sc, f0, f1, add0, add1, sems, sem = rest[-12:]
    i = pl.program_id(0)
    tile = tile_of(i, info)
    panel = tile // (PANEL // TILE)
    inside = tile % (PANEL // TILE) * TILE
    consts = [(w0_at, w0), (w1_at, w1), (v_at, v), (sc_at, sc), (f0_at, f0), (f1_at, f1)]
    fetches = copies(consts, sems)

    @pl.when(i == 0)
    def _():
        start(fetches)

    for k, source, target in ((1, r0, add0), (2, r1, add1)):
        @pl.when(panel == info[k])
        def _(source=source, target=target):
            copy = pltpu.make_async_copy(source.at[pl.ds(inside, TILE)], target, sem)
            copy.start()
            copy.wait()

    @pl.when(i == 0)
    def _():
        wait(fetches[:1])

    xs = jnp.where(i < pl.num_programs(0) // 2, xa[...], xb[...])
    p0 = dot_nn(xs, w0[...]) * SCALE + jnp.where(panel == info[1], add0[...], 0.0)
    p0 = p0.astype(BF16)
    f_ref[0] = p0

    @pl.when(i == 0)
    def _():
        wait(fetches[1:3])

    p1 = dot_nn(xs, w1[...]) * SCALE + jnp.where(panel == info[2], add1[...], 0.0)
    p1 = (p1 - dot_nn(p0, v[...])).astype(BF16)
    f_ref[1] = p1

    @pl.when(i == 0)
    def _():
        wait(fetches[3:])

    row = lax.broadcasted_iota(jnp.int32, (TILE, PANEL), 0) + inside
    diagonal = row == lax.broadcasted_iota(jnp.int32, (TILE, PANEL), 1)
    ridge = jnp.where(diagonal & (panel == info[3]), gc[...], 0.0)
    t = dot_nn(xs, sc[...]) * SCALE + ridge - dot_nn(p0, f0[...]) - dot_nn(p1, f1[...])
    t_ref[...] = jnp.where(info[4] == 1, 0.0, t)


def tile_of(i, info):
    each = pl.num_programs(0) // 2
    return (info[0] ^ (i // each)) * (S // TILE) + info[5] + i % each


def finish(info, xs, gc, consts, prior=()):
    hbm = pl.BlockSpec(memory_space=pl.ANY)
    each = xs[0].shape[0] // TILE
    at = 2 + len(xs) + len(consts)

    def tile(i, info):
        return (info[0] ^ (i // each)) * (S // TILE) + info[5] + i % each

    return pl.pallas_call(
        finish_kernel,
        out_shape=(
            jax.ShapeDtypeStruct((4 * S, PANEL), F32),
            jax.ShapeDtypeStruct((2, 4 * S, PANEL), BF16),
        ),
        grid_spec=pltpu.PrefetchScalarGridSpec(
            num_scalar_prefetch=1,
            grid=(2 * each,),
            in_specs=[
                pl.BlockSpec((TILE, S), lambda i, info: (jnp.minimum(i, each - 1), 0)),
                pl.BlockSpec((TILE, S), lambda i, info: (jnp.maximum(i - each, 0), 0)),
            ]
            + [pl.BlockSpec((1, PANEL), lambda i, info: (0, 0))]
            + [hbm] * (len(consts) + len(prior)),
            out_specs=(
                pl.BlockSpec((TILE, PANEL), lambda i, info: (tile(i, info), 0)),
                pl.BlockSpec((2, TILE, PANEL), lambda i, info: (0, tile(i, info), 0)),
            ),
            scratch_shapes=[pltpu.VMEM(value.shape, value.dtype) for value in consts[:6]]
            + [pltpu.VMEM((TILE, PANEL), F32), pltpu.VMEM((TILE, PANEL), F32)]
            + [pltpu.SemaphoreType.DMA((6,)), pltpu.SemaphoreType.DMA],
        ),
        input_output_aliases={at: 0, at + 1: 1} if prior else {},
        compiler_params=pltpu.CompilerParams(vmem_limit_bytes=34 << 20),
        name="finish",
    )(info, *xs, gc, *in_hbm(consts), *prior)


def on_device(samples, whitening, ridge, slab_start, panels):
    col = lax.axis_index("col")
    tm = lax.axis_index("tm")
    row = lax.axis_index("row")
    core = col % 2
    y = (col // 2) * 2 + tm
    slab = slab_start[0]
    half, owner_tm, owner_row = slab % 2, (slab // 2) % 2, slab // 4
    q0, q1 = panels[0], panels[1]
    local = samples[:, :, 0, :]

    def pair(value, bit):
        other = swap(value, bit)
        upper = (col & bit) != 0
        return jnp.stack([jnp.where(upper, other, value), jnp.where(upper, value, other)])

    mine = lax.dynamic_index_in_dim(local, owner_row, 1, keepdims=False)
    chip = pair(mine, 1)

    def panel_of(values, q):
        start = (q // 2, 0, (q % 2) * PANEL)
        return lax.dynamic_slice(values, start, (1, values.shape[1], PANEL))[0]

    wanted = jnp.stack([panel_of(chip, jnp.where(core == 0, q0, q1)), panel_of(chip, core), panel_of(chip, core + 2)])
    wanted, ridge_sent = lax.optimization_barrier((wanted, ridge))
    away = (y - (half * 2 + owner_tm)) % 4
    part = wanted
    for k in range(1, 4):
        got = lax.ppermute(wanted, ("col", "tm"), y_shift(k))
        part = jnp.where(away == k, got, part)
    ridges = lax.dynamic_update_index_in_dim(jnp.zeros((4, PANEL), F32), ridge_sent, col, 0)
    for bit in (1, 2, 3):
        ridges = lax.dynamic_update_index_in_dim(ridges, swap(ridge_sent, bit), col ^ bit, 0)
    part, ridges = lax.optimization_barrier((part, ridges))
    own_part = jnp.where(col // 2 == 0, part[1], part[2])
    own_raw = lax.all_gather(own_part, "row", axis=0, tiled=True)
    line = ring_gather(part[0], "row", z_shift, row % 4).reshape(S // 4, PANEL)
    pieces = [line] + [lax.ppermute(line, "row", x_shift(k)) for k in range(1, 4)]
    g0 = lax.dynamic_slice_in_dim(ridges, q0, 1, 0)
    g1 = lax.dynamic_slice_in_dim(ridges, q1, 1, 0)
    pieces[1], local = lax.optimization_barrier((pieces[1], local))
    total = 0.0
    for k, piece in enumerate(pieces):
        columns = (row // 4 - k) % 4 * (S // 4)
        total = total + dot_nn(lax.dynamic_slice_in_dim(whitening, columns, S // 4, 1), piece)
    pivot = total.astype(BF16)
    other = swap(pivot, 1)

    moved = lax.all_to_all(local, "row", split_axis=1, concat_axis=0, tiled=True)
    which = core.astype(jnp.int32)[None]
    inv0, u, r0 = chain0(which, pivot, other, g0)
    moved, own_raw, inv0, u = lax.optimization_barrier((moved, own_raw, inv0, u))
    own = lax.dot_general(
        moved.reshape(S, S), whitening, (((0,), (1,)), ((), ())), preferred_element_type=F32
    ).astype(BF16)
    far0, far1 = swap(own[:PANEL], 2), swap(own[PANEL:], 2)
    near = swap(own, 1)
    own, u = lax.optimization_barrier((own, u))
    w1, v, f1, r1, w0, sc, f0 = chain1(which, pivot, other, own_raw, whitening, g1, inv0, u)
    far0, w1 = lax.optimization_barrier((far0, w1))

    holds = (row == owner_row) & (tm == owner_tm)
    done = (col == q0) | (col == q1)

    def slab_tile(q):
        return jnp.where(holds, half * 4 + q, -1)

    def info(c, tile):
        flags = [c, slab_tile(q0), slab_tile(q1), slab_tile(col), done, jnp.int32(tile)]
        return jnp.stack([flag.astype(jnp.int32) for flag in flags])

    consts = (w0, w1, v, sc, f0, f1, r0, r1)
    gc = ridge[None, :]
    out = finish(info(col, 0), (own, near), gc, consts)
    far1, out = lax.optimization_barrier((far1, out))
    out = finish(info(col ^ 2, 0), (far0, swap(far0, 1)), gc, consts, out)
    return finish(info(col ^ 2, PANEL // TILE), (far1, swap(far1, 1)), gc, consts, out)


def solution(mesh):
    in_specs = (P("row", None, "tm", "col"), P(), P("col"), P(), P())
    out_specs = (P(("row", "tm"), "col"), P(None, ("row", "tm"), None))
    return jax.shard_map(
        on_device, mesh=mesh, in_specs=in_specs, out_specs=out_specs, check_vma=False
    )
```

```python
import jax
import jax.numpy as jnp
from jax import lax
from jax.experimental import pallas as pl
from jax.experimental.pallas import tpu as pltpu
from jax.sharding import PartitionSpec as P

S = 1024
PANEL = 512
TILE = 512
BLOCK = 128
SCALE = 1.0 / 32.0
HIGH = lax.Precision.HIGHEST
F32 = jnp.float32
BF16 = jnp.bfloat16


def place(y, core):
    return ((y // 2) * 2 + core) * 2 + y % 2


def y_shift(k):
    return [(place(y, m), place((y + k) % 4, m)) for y in range(4) for m in range(2)]


def x_shift(k):
    return [(x * 4 + z, ((x + k) % 4) * 4 + z) for x in range(4) for z in range(4)]


def z_shift(k):
    return [(x * 4 + z, x * 4 + (z + k) % 4) for x in range(4) for z in range(4)]


def swap(value, bit):
    return lax.ppermute(value, "col", [(c, c ^ bit) for c in range(4)])


def ring_gather(piece, axis, shift, own):
    full = jnp.zeros((4,) + piece.shape, piece.dtype)
    full = lax.dynamic_update_index_in_dim(full, piece, own, 0)
    for k in range(1, 4):
        got = lax.ppermute(piece, axis, shift(k))
        full = lax.dynamic_update_index_in_dim(full, got, (own - k) % 4, 0)
    return full


def dot_nn(a, b):
    return jnp.dot(a, b, preferred_element_type=F32)


def dot_tn(a, b, precision=None):
    return lax.dot_general(
        a, b, (((0,), (0,)), ((), ())), precision=precision, preferred_element_type=F32
    )


def dot_nt(a, b):
    return lax.dot_general(a, b, (((1,), (1,)), ((), ())), preferred_element_type=F32)


def halves(value):
    high = value.astype(BF16)
    return high, (value - high.astype(F32)).astype(BF16)


def thirds(value):
    high = value.astype(BF16).astype(F32)
    rest = value - high
    middle = rest.astype(BF16).astype(F32)
    return high, middle, rest - middle


def outer(rows):
    h, m, l = thirds(rows)
    w = BLOCK
    left = jnp.concatenate([h[:, :w], h[:, :w], m[:, :w], m[:, :w], h[:, :w], l[:, :w]], 0)
    right = jnp.concatenate([h, m, h, m, l, h], 0)
    return dot_tn(left.astype(BF16), right.astype(BF16))


def factor_block(w, spare):
    sub = lax.broadcasted_iota(jnp.int32, (8, BLOCK), 0)
    lane = lax.broadcasted_iota(jnp.int32, (8, BLOCK), 1)
    left, right = w[:8, :BLOCK], w[:8, BLOCK:]
    for k in range(0, BLOCK, 8):
        d = {}
        for j in range(8):
            column = jnp.broadcast_to(left[:, k + j : k + j + 1], (8, BLOCK))
            for i in range(j, 8):
                d[i, j] = jnp.broadcast_to(column[i : i + 1, :], (8, BLOCK))
        lefts, rights = [], []
        for j in range(8):
            r = lax.rsqrt(d[j, j])
            for i in range(j + 1, 8):
                d[i, j] = d[i, j] * r
            for i in range(j + 1, 8):
                for n in range(i, 8):
                    d[n, i] = d[n, i] - d[n, j] * d[i, j]
            a = jnp.broadcast_to(left[j : j + 1, :], (8, BLOCK))
            b = jnp.broadcast_to(right[j : j + 1, :], (8, BLOCK))
            for i in range(j):
                a = a - d[j, i] * lefts[i]
                b = b - d[j, i] * rights[i]
            lefts.append(a * r)
            rights.append(b * r)
        new_left = jnp.zeros((8, BLOCK), F32)
        new_right = jnp.zeros((8, BLOCK), F32)
        for j in range(8):
            new_left = jnp.where(sub == j, lefts[j], new_left)
            new_right = jnp.where(sub == j, rights[j], new_right)
        n = k + 8
        if n < BLOCK:
            left, right = w[n : n + 8, :BLOCK], w[n : n + 8, BLOCK:]
            at = lane == sub + n
            for j in range(8):
                c = jnp.sum(jnp.where(at, lefts[j], 0.0), axis=1, keepdims=True)
                left = left - c * lefts[j]
                right = right - c * rights[j]
        w[k:n, :BLOCK] = new_left
        w[k:n, BLOCK:] = new_right
        if n + 8 < BLOCK:
            update = outer(jnp.concatenate([new_left, new_right], 1))
            w[n + 8 :, :] = w[n + 8 :, :] - update[n + 8 :, :]
        if spare and k % 32 == 0:
            spare.pop(0)()


def eye(n):
    return lax.broadcasted_iota(jnp.int32, (n, n), 0) == lax.broadcasted_iota(jnp.int32, (n, n), 1)


def eliminate(m, w, spare):
    extra = m.shape[1] - PANEL
    for r0 in range(0, PANEL, BLOCK):
        r1 = r0 + BLOCK
        w[:, :BLOCK] = m[r0:r1, r0:r1]
        w[:, BLOCK:] = eye(BLOCK).astype(F32)
        factor_block(w, spare)
        rows = jnp.dot(w[:, BLOCK:], m[r0:r1, r1 : extra + r1], precision=HIGH)
        m[r0:r1, r1 : extra + r1] = rows
        if r1 < PANEL:
            m[r1:, r1 : extra + r1] -= dot_tn(rows[:, : PANEL - r1], rows, HIGH)


def copies(pairs, sems):
    return [pltpu.make_async_copy(a, b, sems.at[k]) for k, (a, b) in enumerate(pairs)]


def in_hbm(values):
    return [pltpu.with_memory_space_constraint(value, pltpu.HBM) for value in values]


def start(transfers):
    for transfer in transfers:
        transfer.start()


def wait(transfers):
    for transfer in transfers:
        transfer.wait()


def order_panels(core, mine, other, s0, s1):
    s0[...] = jnp.where(core[0] == 0, mine[...], other[...])
    s1[...] = jnp.where(core[0] == 0, other[...], mine[...])


def chain0_kernel(
    core, g0, mine, other, inv0_at, u_at, r0_at, m0, w, s0, s1, inv0, u, r0, outs
):
    order_panels(core, mine, other, s0, s1)
    unit = eye(PANEL)
    m0[:, 2 * PANEL :] = unit.astype(F32)
    m0[:, :PANEL] = dot_tn(s0[...], s0[...]) * SCALE + jnp.where(unit, g0[...], 0.0)
    m0[:, PANEL : 2 * PANEL] = dot_tn(s0[...], s1[...]) * SCALE
    eliminate(m0, w, [])
    inv0[...] = m0[:, 2 * PANEL :]
    u[...] = m0[:, PANEL : 2 * PANEL].astype(BF16)
    r0[...] = (m0[:, 2 * PANEL :] * g0[...]).T
    stores = copies([(inv0, inv0_at), (u, u_at), (r0, r0_at)], outs)
    start(stores)
    wait(stores)


def chain0(core, mine, other, g0):
    hbm = pl.BlockSpec(memory_space=pltpu.HBM)
    square = pltpu.HBM((PANEL, PANEL), F32)
    return pl.pallas_call(
        chain0_kernel,
        out_shape=(square, pltpu.HBM((PANEL, PANEL), BF16), square),
        in_specs=[pl.BlockSpec(memory_space=pltpu.SMEM)]
        + [pl.BlockSpec(memory_space=pltpu.VMEM)] * 3,
        out_specs=[hbm] * 3,
        scratch_shapes=[
            pltpu.VMEM((PANEL, 3 * PANEL), F32),
            pltpu.VMEM((BLOCK, 2 * BLOCK), F32),
            pltpu.VMEM((S, PANEL), BF16),
            pltpu.VMEM((S, PANEL), BF16),
            pltpu.VMEM((PANEL, PANEL), F32),
            pltpu.VMEM((PANEL, PANEL), BF16),
            pltpu.VMEM((PANEL, PANEL), F32),
            pltpu.SemaphoreType.DMA((3,)),
        ],
        compiler_params=pltpu.CompilerParams(vmem_limit_bytes=15 << 20),
        cost_estimate=pl.CostEstimate(flops=10**6, transcendentals=0, bytes_accessed=1 << 10),
        name="chain0",
    )(core, g0, mine, other)


def chain1_kernel(
    core, g1, mine, other, inv0_at, u_at, raw_at, whitening_at,
    w0, w1, sc, small, r1_at, m1, e1, w, s0, s1, inv0, u, raw, whitening, r1, ins, out,
):
    fetches = copies(
        [(u_at, u), (whitening_at, whitening), (raw_at, raw), (inv0_at, inv0)], ins
    )
    start(fetches)
    order_panels(core, mine, other, s0, s1)
    unit = eye(PANEL)
    m1[:, PANEL:] = unit.astype(F32)
    m1[:, :PANEL] = dot_tn(s1[...], s1[...]) * SCALE + jnp.where(unit, g1[...], 0.0)
    wait(fetches[:1])
    m1[:, :PANEL] -= dot_tn(u[...], u[...])

    def whiten(at):
        def run():
            if at == 0:
                wait(fetches[1:3])
            sc[:, at : at + BLOCK] = dot_nn(whitening[...], raw[:, at : at + BLOCK]).astype(BF16)
        return run

    def coupling(at):
        def run():
            if at == 0:
                wait(fetches[3:])
            h0, l0 = halves(inv0[...])
            part = sc[:, at : at + BLOCK]
            eh, el = halves(dot_tn(s0[...], part) * SCALE)
            c0 = (dot_nn(h0, eh) + dot_nn(h0, el) + dot_nn(l0, eh)).astype(BF16)
            small[PANEL : 2 * PANEL, at : at + BLOCK] = c0
            e1[:, at : at + BLOCK] = dot_tn(s1[...], part) * SCALE - dot_tn(u[...], c0)
        return run

    def product(at):
        def run():
            h0, l0 = halves(inv0[...])
            rows = s0[at : at + BLOCK, :]
            w0[at : at + BLOCK, :] = (dot_nt(rows, h0) + dot_nt(rows, l0)).astype(BF16)
        return run

    spare = [whiten(at) for at in range(0, PANEL, BLOCK)]
    spare += [coupling(at) for at in range(0, PANEL, BLOCK)]
    spare += [product(at) for at in range(0, S, BLOCK)]
    eliminate(m1, w, spare)
    r1[...] = (m1[:, PANEL:] * g1[...]).T
    store = copies([(r1, r1_at)], out)
    start(store)
    h1, l1 = halves(m1[:, PANEL:])
    w1[...] = (dot_nt(s1[...], h1) + dot_nt(s1[...], l1)).astype(BF16)
    small[:PANEL, :] = (dot_nt(u[...], h1) + dot_nt(u[...], l1)).astype(BF16)
    eh, el = halves(e1[...])
    small[2 * PANEL :, :] = (dot_nn(h1, eh) + dot_nn(h1, el) + dot_nn(l1, eh)).astype(BF16)
    wait(store)


def chain1(core, mine, other, raw, whitening, g1, inv0, u):
    hbm = pl.BlockSpec(memory_space=pl.ANY)
    vmem = pl.BlockSpec(memory_space=pltpu.VMEM)
    small = jax.ShapeDtypeStruct((3 * PANEL, PANEL), BF16)
    tall = jax.ShapeDtypeStruct((S, PANEL), BF16)
    return pl.pallas_call(
        chain1_kernel,
        out_shape=(tall, tall, tall, small, pltpu.HBM((PANEL, PANEL), F32)),
        in_specs=[pl.BlockSpec(memory_space=pltpu.SMEM)] + [vmem] * 3 + [hbm] * 4,
        out_specs=[vmem] * 4 + [hbm],
        scratch_shapes=[
            pltpu.VMEM((PANEL, 2 * PANEL), F32),
            pltpu.VMEM((PANEL, PANEL), F32),
            pltpu.VMEM((BLOCK, 2 * BLOCK), F32),
            pltpu.VMEM((S, PANEL), BF16),
            pltpu.VMEM((S, PANEL), BF16),
            pltpu.VMEM((PANEL, PANEL), F32),
            pltpu.VMEM((PANEL, PANEL), BF16),
            pltpu.VMEM((S, PANEL), BF16),
            pltpu.VMEM((S, S), BF16),
            pltpu.VMEM((PANEL, PANEL), F32),
            pltpu.SemaphoreType.DMA((4,)),
            pltpu.SemaphoreType.DMA((1,)),
        ],
        compiler_params=pltpu.CompilerParams(vmem_limit_bytes=17 << 20),
        cost_estimate=pl.CostEstimate(flops=35 * 10**9, transcendentals=0, bytes_accessed=8 << 20),
        name="chain1",
    )(core, g1, mine, other, *in_hbm((inv0, u, raw, whitening)))


def finish_kernel(info, xa, xb, gc, w0, w1, sc, small, r0, r1, *rest):
    t_ref, f_ref, add0, add1, sems = rest[-5:]
    i = pl.program_id(0)
    tile = tile_of(i, info)
    panel = tile // (PANEL // TILE)
    inside = tile % (PANEL // TILE) * TILE

    @pl.when((i == 0) & (info[1] >= 0))
    def _():
        fetches = copies([(r0, add0), (r1, add1)], sems)
        start(fetches)
        wait(fetches)

    xs = jnp.where(i < pl.num_programs(0) // 2, xa[...], xb[...])
    p0 = dot_nn(xs, w0[...]) * SCALE + jnp.where(panel == info[1], add0[...], 0.0)
    p0 = p0.astype(BF16)
    f_ref[0] = p0

    p1 = dot_nn(xs, w1[...]) * SCALE + jnp.where(panel == info[2], add1[...], 0.0)
    p1 = (p1 - dot_nn(p0, small[:PANEL, :])).astype(BF16)
    f_ref[1] = p1

    row = lax.broadcasted_iota(jnp.int32, (TILE, PANEL), 0) + inside
    diagonal = row == lax.broadcasted_iota(jnp.int32, (TILE, PANEL), 1)
    ridge = jnp.where(diagonal & (panel == info[3]), gc[...], 0.0)
    t = dot_nn(xs, sc[...]) * SCALE + ridge
    t = t - dot_nn(p0, small[PANEL : 2 * PANEL, :]) - dot_nn(p1, small[2 * PANEL :, :])
    t_ref[...] = jnp.where(info[4] == 1, 0.0, t)


def tile_of(i, info):
    each = pl.num_programs(0) // 2
    return (info[0] ^ (i // each)) * (S // TILE) + info[5] + i % each


def finish(info, xs, gc, consts, prior=()):
    hbm = pl.BlockSpec(memory_space=pl.ANY)
    each = xs[0].shape[0] // TILE
    at = 2 + len(xs) + len(consts)

    def tile(i, info):
        return (info[0] ^ (i // each)) * (S // TILE) + info[5] + i % each

    return pl.pallas_call(
        finish_kernel,
        out_shape=(
            jax.ShapeDtypeStruct((4 * S, PANEL), F32),
            jax.ShapeDtypeStruct((2, 4 * S, PANEL), BF16),
        ),
        grid_spec=pltpu.PrefetchScalarGridSpec(
            num_scalar_prefetch=1,
            grid=(2 * each,),
            in_specs=[
                pl.BlockSpec((TILE, S), lambda i, info: (jnp.minimum(i, each - 1), 0)),
                pl.BlockSpec((TILE, S), lambda i, info: (jnp.maximum(i - each, 0), 0)),
            ]
            + [pl.BlockSpec((1, PANEL), lambda i, info: (0, 0))]
            + [pl.BlockSpec(memory_space=pltpu.VMEM)] * 4
            + [hbm] * (len(consts) - 4 + len(prior)),
            out_specs=(
                pl.BlockSpec((TILE, PANEL), lambda i, info: (tile(i, info), 0)),
                pl.BlockSpec((2, TILE, PANEL), lambda i, info: (0, tile(i, info), 0)),
            ),
            scratch_shapes=[
                pltpu.VMEM((PANEL, PANEL), F32),
                pltpu.VMEM((PANEL, PANEL), F32),
                pltpu.SemaphoreType.DMA((2,)),
            ],
        ),
        input_output_aliases={at: 0, at + 1: 1} if prior else {},
        compiler_params=pltpu.CompilerParams(vmem_limit_bytes=17 << 20),
        name="finish",
    )(info, *xs, gc, *consts[:4], *in_hbm(consts[4:]), *prior)


def on_device(samples, whitening, ridge, slab_start, panels):
    col = lax.axis_index("col")
    tm = lax.axis_index("tm")
    row = lax.axis_index("row")
    core = col % 2
    y = (col // 2) * 2 + tm
    slab = slab_start[0]
    half, owner_tm, owner_row = slab % 2, (slab // 2) % 2, slab // 4
    q0, q1 = panels[0], panels[1]
    local = samples[:, :, 0, :]

    def pair(value, bit):
        other = swap(value, bit)
        upper = (col & bit) != 0
        return jnp.stack([jnp.where(upper, other, value), jnp.where(upper, value, other)])

    mine = lax.dynamic_index_in_dim(local, owner_row, 1, keepdims=False)
    chip = pair(mine, 1)

    def panel_of(values, q):
        start = (q // 2, 0, (q % 2) * PANEL)
        return lax.dynamic_slice(values, start, (1, values.shape[1], PANEL))[0]

    wanted = jnp.stack([panel_of(chip, jnp.where(core == 0, q0, q1)), panel_of(chip, core), panel_of(chip, core + 2)])
    wanted, ridge_sent = lax.optimization_barrier((wanted, ridge))
    away = (y - (half * 2 + owner_tm)) % 4
    part = wanted
    for k in range(1, 4):
        got = lax.ppermute(wanted, ("col", "tm"), y_shift(k))
        part = jnp.where(away == k, got, part)
    ridges = lax.dynamic_update_index_in_dim(jnp.zeros((4, PANEL), F32), ridge_sent, col, 0)
    for bit in (1, 2, 3):
        ridges = lax.dynamic_update_index_in_dim(ridges, swap(ridge_sent, bit), col ^ bit, 0)
    part, ridges = lax.optimization_barrier((part, ridges))
    own_part = jnp.where(col // 2 == 0, part[1], part[2])
    own_raw = lax.all_gather(own_part, "row", axis=0, tiled=True)
    line = ring_gather(part[0], "row", z_shift, row % 4).reshape(S // 4, PANEL)
    pieces = [line] + [lax.ppermute(line, "row", x_shift(k)) for k in range(1, 4)]
    g0 = lax.dynamic_slice_in_dim(ridges, q0, 1, 0)
    g1 = lax.dynamic_slice_in_dim(ridges, q1, 1, 0)
    pieces[1], local = lax.optimization_barrier((pieces[1], local))
    total = 0.0
    for k, piece in enumerate(pieces):
        columns = (row // 4 - k) % 4 * (S // 4)
        total = total + dot_nn(lax.dynamic_slice_in_dim(whitening, columns, S // 4, 1), piece)
    pivot = total.astype(BF16)
    other = swap(pivot, 1)

    moved = lax.all_to_all(local, "row", split_axis=1, concat_axis=0, tiled=True)
    which = core.astype(jnp.int32)[None]
    inv0, u, r0 = chain0(which, pivot, other, g0)
    moved, own_raw, inv0, u = lax.optimization_barrier((moved, own_raw, inv0, u))
    own = lax.dot_general(
        moved.reshape(S, S), whitening, (((0,), (1,)), ((), ())), preferred_element_type=F32
    ).astype(BF16)
    far0, far1 = swap(own[:PANEL], 2), swap(own[PANEL:], 2)
    near = swap(own, 1)
    own, u = lax.optimization_barrier((own, u))
    w0, w1, sc, small, r1 = chain1(which, pivot, other, own_raw, whitening, g1, inv0, u)
    far0, w1 = lax.optimization_barrier((far0, w1))

    holds = (row == owner_row) & (tm == owner_tm)
    done = (col == q0) | (col == q1)

    def slab_tile(q):
        return jnp.where(holds, half * 4 + q, -1)

    def info(c, tile):
        flags = [c, slab_tile(q0), slab_tile(q1), slab_tile(col), done, jnp.int32(tile)]
        return jnp.stack([flag.astype(jnp.int32) for flag in flags])

    consts = (w0, w1, sc, small, r0, r1)
    gc = ridge[None, :]
    out = finish(info(col, 0), (own, near), gc, consts)
    far1, out = lax.optimization_barrier((far1, out))
    out = finish(info(col ^ 2, 0), (far0, swap(far0, 1)), gc, consts, out)
    return finish(info(col ^ 2, PANEL // TILE), (far1, swap(far1, 1)), gc, consts, out)


def solution(mesh):
    in_specs = (P("row", None, "tm", "col"), P(), P("col"), P(), P())
    out_specs = (P(("row", "tm"), "col"), P(None, ("row", "tm"), None))
    return jax.shard_map(
        on_device, mesh=mesh, in_specs=in_specs, out_specs=out_specs, check_vma=False
    )
```

```python
import jax
import jax.numpy as jnp
from jax import lax
from jax.experimental import pallas as pl
from jax.experimental.pallas import tpu as pltpu
from jax.sharding import PartitionSpec as P

S = 1024
PANEL = 512
TILE = 512
BLOCK = 128
SCALE = 1.0 / 32.0
HIGH = lax.Precision.HIGHEST
F32 = jnp.float32
BF16 = jnp.bfloat16


def place(y, core):
    return ((y // 2) * 2 + core) * 2 + y % 2


def y_shift(k):
    return [(place(y, m), place((y + k) % 4, m)) for y in range(4) for m in range(2)]


def x_shift(k):
    return [(x * 4 + z, ((x + k) % 4) * 4 + z) for x in range(4) for z in range(4)]


def z_shift(k):
    return [(x * 4 + z, x * 4 + (z + k) % 4) for x in range(4) for z in range(4)]


def swap(value, bit):
    return lax.ppermute(value, "col", [(c, c ^ bit) for c in range(4)])


def ring_gather(piece, axis, shift, own):
    full = jnp.zeros((4,) + piece.shape, piece.dtype)
    full = lax.dynamic_update_index_in_dim(full, piece, own, 0)
    for k in range(1, 4):
        got = lax.ppermute(piece, axis, shift(k))
        full = lax.dynamic_update_index_in_dim(full, got, (own - k) % 4, 0)
    return full


def dot_nn(a, b):
    return jnp.dot(a, b, preferred_element_type=F32)


def dot_tn(a, b, precision=None):
    return lax.dot_general(
        a, b, (((0,), (0,)), ((), ())), precision=precision, preferred_element_type=F32
    )


def dot_nt(a, b):
    return lax.dot_general(a, b, (((1,), (1,)), ((), ())), preferred_element_type=F32)


def halves(value):
    high = value.astype(BF16)
    return high, (value - high.astype(F32)).astype(BF16)


def thirds(value):
    high = value.astype(BF16).astype(F32)
    rest = value - high
    middle = rest.astype(BF16).astype(F32)
    return high, middle, rest - middle


def outer(rows):
    h, m, l = thirds(rows)
    w = BLOCK
    left = jnp.concatenate([h[:, :w], h[:, :w], m[:, :w], m[:, :w], h[:, :w], l[:, :w]], 0)
    right = jnp.concatenate([h, m, h, m, l, h], 0)
    return dot_tn(left.astype(BF16), right.astype(BF16))


def factor_block(w, spare):
    sub = lax.broadcasted_iota(jnp.int32, (8, BLOCK), 0)
    lane = lax.broadcasted_iota(jnp.int32, (8, BLOCK), 1)
    left, right = w[:8, :BLOCK], w[:8, BLOCK:]
    for k in range(0, BLOCK, 8):
        d = {}
        for j in range(8):
            column = jnp.broadcast_to(left[:, k + j : k + j + 1], (8, BLOCK))
            for i in range(j, 8):
                d[i, j] = jnp.broadcast_to(column[i : i + 1, :], (8, BLOCK))
        lefts, rights = [], []
        for j in range(8):
            r = lax.rsqrt(d[j, j])
            for i in range(j + 1, 8):
                d[i, j] = d[i, j] * r
            for i in range(j + 1, 8):
                for n in range(i, 8):
                    d[n, i] = d[n, i] - d[n, j] * d[i, j]
            a = jnp.broadcast_to(left[j : j + 1, :], (8, BLOCK))
            b = jnp.broadcast_to(right[j : j + 1, :], (8, BLOCK))
            for i in range(j):
                a = a - d[j, i] * lefts[i]
                b = b - d[j, i] * rights[i]
            lefts.append(a * r)
            rights.append(b * r)
        new_left = jnp.zeros((8, BLOCK), F32)
        new_right = jnp.zeros((8, BLOCK), F32)
        for j in range(8):
            new_left = jnp.where(sub == j, lefts[j], new_left)
            new_right = jnp.where(sub == j, rights[j], new_right)
        n = k + 8
        if n < BLOCK:
            left, right = w[n : n + 8, :BLOCK], w[n : n + 8, BLOCK:]
            at = lane == sub + n
            for j in range(8):
                c = jnp.sum(jnp.where(at, lefts[j], 0.0), axis=1, keepdims=True)
                left = left - c * lefts[j]
                right = right - c * rights[j]
        w[k:n, :BLOCK] = new_left
        w[k:n, BLOCK:] = new_right
        if n + 8 < BLOCK:
            update = outer(jnp.concatenate([new_left, new_right], 1))
            w[n + 8 :, :] = w[n + 8 :, :] - update[n + 8 :, :]
        if spare and k % 32 == 0:
            spare.pop(0)()


def eye(n):
    return lax.broadcasted_iota(jnp.int32, (n, n), 0) == lax.broadcasted_iota(jnp.int32, (n, n), 1)


def eliminate(m, w, spare):
    extra = m.shape[1] - PANEL
    for r0 in range(0, PANEL, BLOCK):
        r1 = r0 + BLOCK
        w[:, :BLOCK] = m[r0:r1, r0:r1]
        w[:, BLOCK:] = eye(BLOCK).astype(F32)
        factor_block(w, spare)
        rows = jnp.dot(w[:, BLOCK:], m[r0:r1, r1 : extra + r1], precision=HIGH)
        m[r0:r1, r1 : extra + r1] = rows
        if r1 < PANEL:
            m[r1:, r1 : extra + r1] -= dot_tn(rows[:, : PANEL - r1], rows, HIGH)


def copies(pairs, sems):
    return [pltpu.make_async_copy(a, b, sems.at[k]) for k, (a, b) in enumerate(pairs)]


def in_hbm(values):
    return [pltpu.with_memory_space_constraint(value, pltpu.HBM) for value in values]


def start(transfers):
    for transfer in transfers:
        transfer.start()


def wait(transfers):
    for transfer in transfers:
        transfer.wait()


def order_panels(core, mine, other, s0, s1):
    s0[...] = jnp.where(core[0] == 0, mine[...], other[...])
    s1[...] = jnp.where(core[0] == 0, other[...], mine[...])


def chain0_kernel(
    core, g0, mine, other, inv0_at, u_at, r0_at, m0, w, s0, s1, inv0, u, r0, outs
):
    order_panels(core, mine, other, s0, s1)
    unit = eye(PANEL)
    m0[:, 2 * PANEL :] = unit.astype(F32)
    m0[:, :PANEL] = dot_tn(s0[...], s0[...]) * SCALE + jnp.where(unit, g0[...], 0.0)
    m0[:, PANEL : 2 * PANEL] = dot_tn(s0[...], s1[...]) * SCALE
    eliminate(m0, w, [])
    inv0[...] = m0[:, 2 * PANEL :]
    u[...] = m0[:, PANEL : 2 * PANEL].astype(BF16)
    r0[...] = (m0[:, 2 * PANEL :] * g0[...]).T
    stores = copies([(inv0, inv0_at), (u, u_at), (r0, r0_at)], outs)
    start(stores)
    wait(stores)


def chain0(core, mine, other, g0):
    hbm = pl.BlockSpec(memory_space=pltpu.HBM)
    square = pltpu.HBM((PANEL, PANEL), F32)
    return pl.pallas_call(
        chain0_kernel,
        out_shape=(square, pltpu.HBM((PANEL, PANEL), BF16), square),
        in_specs=[pl.BlockSpec(memory_space=pltpu.SMEM)]
        + [pl.BlockSpec(memory_space=pltpu.VMEM)] * 3,
        out_specs=[hbm] * 3,
        scratch_shapes=[
            pltpu.VMEM((PANEL, 3 * PANEL), F32),
            pltpu.VMEM((BLOCK, 2 * BLOCK), F32),
            pltpu.VMEM((S, PANEL), BF16),
            pltpu.VMEM((S, PANEL), BF16),
            pltpu.VMEM((PANEL, PANEL), F32),
            pltpu.VMEM((PANEL, PANEL), BF16),
            pltpu.VMEM((PANEL, PANEL), F32),
            pltpu.SemaphoreType.DMA((3,)),
        ],
        compiler_params=pltpu.CompilerParams(vmem_limit_bytes=15 << 20),
        cost_estimate=pl.CostEstimate(flops=10**6, transcendentals=0, bytes_accessed=1 << 10),
        name="chain0",
    )(core, g0, mine, other)


def chain1_kernel(
    core, g1, mine, other, inv0_at, u_at, raw_at, whitening_at,
    w0, w1, sc, small, r1_at, m1, e1, w, s0, s1, inv0, u, raw, whitening, r1, ins, out,
):
    fetches = copies(
        [(u_at, u), (whitening_at, whitening), (raw_at, raw), (inv0_at, inv0)], ins
    )
    start(fetches)
    order_panels(core, mine, other, s0, s1)
    unit = eye(PANEL)
    m1[:, PANEL:] = unit.astype(F32)
    m1[:, :PANEL] = dot_tn(s1[...], s1[...]) * SCALE + jnp.where(unit, g1[...], 0.0)
    wait(fetches[:1])
    m1[:, :PANEL] -= dot_tn(u[...], u[...])

    def whiten(at):
        def run():
            if at == 0:
                wait(fetches[1:3])
            sc[:, at : at + BLOCK] = dot_nn(whitening[...], raw[:, at : at + BLOCK]).astype(BF16)
        return run

    def coupling(at):
        def run():
            if at == 0:
                wait(fetches[3:])
            h0, l0 = halves(inv0[...])
            part = sc[:, at : at + BLOCK]
            eh, el = halves(dot_tn(s0[...], part) * SCALE)
            c0 = (dot_nn(h0, eh) + dot_nn(h0, el) + dot_nn(l0, eh)).astype(BF16)
            small[PANEL : 2 * PANEL, at : at + BLOCK] = c0
            e1[:, at : at + BLOCK] = dot_tn(s1[...], part) * SCALE - dot_tn(u[...], c0)
        return run

    def product(at):
        def run():
            h0, l0 = halves(inv0[...])
            rows = s0[at : at + BLOCK, :]
            w0[at : at + BLOCK, :] = (dot_nt(rows, h0) + dot_nt(rows, l0)).astype(BF16)
        return run

    spare = [whiten(at) for at in range(0, PANEL, BLOCK)]
    spare += [coupling(at) for at in range(0, PANEL, BLOCK)]
    spare += [product(at) for at in range(0, S, BLOCK)]
    eliminate(m1, w, spare)
    r1[...] = (m1[:, PANEL:] * g1[...]).T
    store = copies([(r1, r1_at)], out)
    start(store)
    h1, l1 = halves(m1[:, PANEL:])
    w1[...] = (dot_nt(s1[...], h1) + dot_nt(s1[...], l1)).astype(BF16)
    small[:PANEL, :] = (dot_nt(u[...], h1) + dot_nt(u[...], l1)).astype(BF16)
    eh, el = halves(e1[...])
    small[2 * PANEL :, :] = (dot_nn(h1, eh) + dot_nn(h1, el) + dot_nn(l1, eh)).astype(BF16)
    wait(store)


def chain1(core, mine, other, raw, whitening, g1, inv0, u):
    hbm = pl.BlockSpec(memory_space=pl.ANY)
    vmem = pl.BlockSpec(memory_space=pltpu.VMEM)
    small = jax.ShapeDtypeStruct((3 * PANEL, PANEL), BF16)
    tall = jax.ShapeDtypeStruct((S, PANEL), BF16)
    return pl.pallas_call(
        chain1_kernel,
        out_shape=(tall, tall, tall, small, pltpu.HBM((PANEL, PANEL), F32)),
        in_specs=[pl.BlockSpec(memory_space=pltpu.SMEM)] + [vmem] * 3 + [hbm] * 4,
        out_specs=[vmem] * 4 + [hbm],
        scratch_shapes=[
            pltpu.VMEM((PANEL, 2 * PANEL), F32),
            pltpu.VMEM((PANEL, PANEL), F32),
            pltpu.VMEM((BLOCK, 2 * BLOCK), F32),
            pltpu.VMEM((S, PANEL), BF16),
            pltpu.VMEM((S, PANEL), BF16),
            pltpu.VMEM((PANEL, PANEL), F32),
            pltpu.VMEM((PANEL, PANEL), BF16),
            pltpu.VMEM((S, PANEL), BF16),
            pltpu.VMEM((S, S), BF16),
            pltpu.VMEM((PANEL, PANEL), F32),
            pltpu.SemaphoreType.DMA((4,)),
            pltpu.SemaphoreType.DMA((1,)),
        ],
        compiler_params=pltpu.CompilerParams(vmem_limit_bytes=17 << 20),
        cost_estimate=pl.CostEstimate(flops=35 * 10**9, transcendentals=0, bytes_accessed=8 << 20),
        name="chain1",
    )(core, g1, mine, other, *in_hbm((inv0, u, raw, whitening)))


def finish_kernel(info, xa, xb, gc, w0, w1, sc, small, r0, r1, *rest):
    t_ref, f_ref, add0, add1, sems = rest[-5:]
    i = pl.program_id(0)
    tile = tile_of(i, info)
    panel = tile // (PANEL // TILE)
    inside = tile % (PANEL // TILE) * TILE

    @pl.when((i == 0) & (info[1] >= 0))
    def _():
        fetches = copies([(r0, add0), (r1, add1)], sems)
        start(fetches)
        wait(fetches)

    xs = jnp.where(i < pl.num_programs(0) // 2, xa[...], xb[...])
    p0 = dot_nn(xs, w0[...]) * SCALE + jnp.where(panel == info[1], add0[...], 0.0)
    p0 = p0.astype(BF16)
    f_ref[0] = p0

    p1 = dot_nn(xs, w1[...]) * SCALE + jnp.where(panel == info[2], add1[...], 0.0)
    p1 = (p1 - dot_nn(p0, small[:PANEL, :])).astype(BF16)
    f_ref[1] = p1

    row = lax.broadcasted_iota(jnp.int32, (TILE, PANEL), 0) + inside
    diagonal = row == lax.broadcasted_iota(jnp.int32, (TILE, PANEL), 1)
    ridge = jnp.where(diagonal & (panel == info[3]), gc[...], 0.0)
    t = dot_nn(xs, sc[...]) * SCALE + ridge
    t = t - dot_nn(p0, small[PANEL : 2 * PANEL, :]) - dot_nn(p1, small[2 * PANEL :, :])
    t_ref[...] = jnp.where(info[4] == 1, 0.0, t)


def tile_of(i, info):
    each = pl.num_programs(0) // 2
    return (info[0] ^ (i // each)) * (S // TILE) + info[5] + i % each


def finish(info, xs, gc, consts, prior=()):
    hbm = pl.BlockSpec(memory_space=pl.ANY)
    each = xs[0].shape[0] // TILE
    at = 2 + len(xs) + len(consts)

    def tile(i, info):
        return (info[0] ^ (i // each)) * (S // TILE) + info[5] + i % each

    return pl.pallas_call(
        finish_kernel,
        out_shape=(
            jax.ShapeDtypeStruct((4 * S, PANEL), F32),
            jax.ShapeDtypeStruct((2, 4 * S, PANEL), BF16),
        ),
        grid_spec=pltpu.PrefetchScalarGridSpec(
            num_scalar_prefetch=1,
            grid=(2 * each,),
            in_specs=[
                pl.BlockSpec((TILE, S), lambda i, info: (jnp.minimum(i, each - 1), 0)),
                pl.BlockSpec((TILE, S), lambda i, info: (jnp.maximum(i - each, 0), 0)),
            ]
            + [pl.BlockSpec((1, PANEL), lambda i, info: (0, 0))]
            + [pl.BlockSpec(memory_space=pltpu.VMEM)] * 4
            + [hbm] * (len(consts) - 4 + len(prior)),
            out_specs=(
                pl.BlockSpec((TILE, PANEL), lambda i, info: (tile(i, info), 0)),
                pl.BlockSpec((2, TILE, PANEL), lambda i, info: (0, tile(i, info), 0)),
            ),
            scratch_shapes=[
                pltpu.VMEM((PANEL, PANEL), F32),
                pltpu.VMEM((PANEL, PANEL), F32),
                pltpu.SemaphoreType.DMA((2,)),
            ],
        ),
        input_output_aliases={at: 0, at + 1: 1} if prior else {},
        compiler_params=pltpu.CompilerParams(vmem_limit_bytes=17 << 20),
        name="finish",
    )(info, *xs, gc, *consts[:4], *in_hbm(consts[4:]), *prior)


def on_device(samples, whitening, ridge, slab_start, panels):
    col = lax.axis_index("col")
    tm = lax.axis_index("tm")
    row = lax.axis_index("row")
    core = col % 2
    y = (col // 2) * 2 + tm
    slab = slab_start[0]
    half, owner_tm, owner_row = slab % 2, (slab // 2) % 2, slab // 4
    q0, q1 = panels[0], panels[1]
    local = samples[:, :, 0, :]

    def pair(value, bit):
        other = swap(value, bit)
        upper = (col & bit) != 0
        return jnp.stack([jnp.where(upper, other, value), jnp.where(upper, value, other)])

    mine = lax.dynamic_index_in_dim(local, owner_row, 1, keepdims=False)
    chip = pair(mine, 1)

    def panel_of(values, q):
        start = (q // 2, 0, (q % 2) * PANEL)
        return lax.dynamic_slice(values, start, (1, values.shape[1], PANEL))[0]

    wanted = jnp.stack([panel_of(chip, jnp.where(core == 0, q0, q1)), panel_of(chip, core), panel_of(chip, core + 2)])
    wanted, ridge_sent = lax.optimization_barrier((wanted, ridge))
    away = (y - (half * 2 + owner_tm)) % 4
    part = wanted
    for k in range(1, 4):
        got = lax.ppermute(wanted, ("col", "tm"), y_shift(k))
        part = jnp.where(away == k, got, part)
    ridges = lax.dynamic_update_index_in_dim(jnp.zeros((4, PANEL), F32), ridge_sent, col, 0)
    for bit in (1, 2, 3):
        ridges = lax.dynamic_update_index_in_dim(ridges, swap(ridge_sent, bit), col ^ bit, 0)
    part, ridges = lax.optimization_barrier((part, ridges))
    own_part = jnp.where(col // 2 == 0, part[1], part[2])
    own_raw = lax.all_gather(own_part, "row", axis=0, tiled=True)
    line = ring_gather(part[0], "row", z_shift, row % 4).reshape(S // 4, PANEL)
    pieces = [line] + [lax.ppermute(line, "row", x_shift(k)) for k in range(1, 4)]
    g0 = lax.dynamic_slice_in_dim(ridges, q0, 1, 0)
    g1 = lax.dynamic_slice_in_dim(ridges, q1, 1, 0)
    total = 0.0
    for k, piece in enumerate(pieces):
        columns = (row // 4 - k) % 4 * (S // 4)
        total = total + dot_nn(lax.dynamic_slice_in_dim(whitening, columns, S // 4, 1), piece)
    pivot = total.astype(BF16)
    other = swap(pivot, 1)

    moved = lax.all_to_all(local, "row", split_axis=1, concat_axis=0, tiled=True)
    which = core.astype(jnp.int32)[None]
    own = lax.dot_general(
        moved.reshape(S, S), whitening, (((0,), (1,)), ((), ())), preferred_element_type=F32
    ).astype(BF16)
    far, near = swap(own, 2), swap(own, 1)
    pivot = lax.optimization_barrier((pivot, own))[0]
    inv0, u, r0 = chain0(which, pivot, other, g0)
    w0, w1, sc, small, r1 = chain1(which, pivot, other, own_raw, whitening, g1, inv0, u)
    far, w1 = lax.optimization_barrier((far, w1))

    holds = (row == owner_row) & (tm == owner_tm)
    done = (col == q0) | (col == q1)

    def slab_tile(q):
        return jnp.where(holds, half * 4 + q, -1)

    def info(c, tile):
        flags = [c, slab_tile(q0), slab_tile(q1), slab_tile(col), done, jnp.int32(tile)]
        return jnp.stack([flag.astype(jnp.int32) for flag in flags])

    consts = (w0, w1, sc, small, r0, r1)
    gc = ridge[None, :]
    out = finish(info(col, 0), (own, near), gc, consts)
    return finish(info(col ^ 2, 0), (far, swap(far, 1)), gc, consts, out)


def solution(mesh):
    in_specs = (P("row", None, "tm", "col"), P(), P("col"), P(), P())
    out_specs = (P(("row", "tm"), "col"), P(None, ("row", "tm"), None))
    return jax.shard_map(
        on_device, mesh=mesh, in_specs=in_specs, out_specs=out_specs, check_vma=False
    )
```
